32 devices in a mesh: row: 4 (over z), col: 8 (over y, x, core).
Axes of the slice: x: 2, y: 2, z: 4, core: 2. Of those that a mesh axis runs over, the one named last changes fastest.
Arguments:
- hessian: float32 [16384, 4, 8, 512], P('row', None, 'col'), may hold values from -1 to 16, as said below
- weights: bfloat16 [512, 16384], P('col', 'row'), may hold values from -6 to 6
- codes: int32 [512, 8192], P('col', 'row'), may hold values from 0 to 255
- tile_map: int32 [32, 64], P('col', 'row'), may hold values from 0 to 511
- codebooks: float32 [512, 2, 256], replicated, may hold values from -6 to 6
Outputs:
- adjusted_codebooks: float32 [512, 2, 256], replicated
The draws below stay inside these ranges and needn't reach their ends.
Inputs may be any that keep to these rules, and one draw needn't show every extreme that they name: `hessian`: H is symmetric with a dominant positive diagonal.
All inputs are finite; a program needn't handle non-finite values.
Results may differ from the reference program's by a relative error of at most 0.0003.
Values sent between devices are 32-bit elements; how exact they have to be, the bound alone decides.
A program may use at most 192 MiB of HBM per device.

```python
import math
import jax
import jax.numpy as jnp
from jax import lax

D = 16384
R = 512
CODES = 256
NB = 512
TILE_ROWS = 16
TILE_COLS = 256
STEPS = 2
N_ROW = 4
N_COL = 8


def draw_hessian(key, part):
    base_key = jax.random.fold_in(key, 23)
    scale_key, noise_key, diag_key = jax.random.split(base_key, 3)
    scales = jnp.exp(jax.random.uniform(scale_key, (D,), jnp.float32, math.log(0.5), math.log(2.0)))
    noise = jnp.clip(jax.random.normal(noise_key, (D, D), jnp.float32), -5.0, 5.0)
    damping = jax.random.uniform(diag_key, (D,), jnp.float32, 1.0, 1.5)
    symmetric = (noise + noise.T) * (0.3 / math.sqrt(2.0 * D))
    eye = (lax.broadcasted_iota(jnp.int32, (D, D), 0) == lax.broadcasted_iota(jnp.int32, (D, D), 1)).astype(jnp.float32)
    inner = symmetric + eye * damping[:, None]
    outer = scales[:, None] * scales[None, :]
    values = outer * inner
    return values.reshape(D, N_ROW, N_COL, D // (N_ROW * N_COL))


def touch_ends(result, stream_key, low, top_value):
    longest = result.shape.index(max(result.shape))
    spots = []
    for shift in (0, 1):
        where = [jax.random.randint(jax.random.fold_in(stream_key, axis), (), 0, length) for axis, length in enumerate(result.shape)]
        where[longest] = (where[longest] + shift) % result.shape[longest]
        spots.append(tuple(where))
    return result.at[spots[0]].set(low).at[spots[1]].set(top_value)


def block_levels(rng, dims, cuts, least, largest):
    def one(dim, blocks):
        steps = jax.random.uniform(jax.random.fold_in(jax.random.fold_in(rng, 6), dim), (blocks,), jnp.float32, least / len(cuts), largest / len(cuts))
        return jnp.repeat(jnp.exp(steps), dims[dim] // blocks).reshape((-1,) + (1,) * (len(dims) - dim - 1))

    gain = one(*cuts[0])
    for cut in cuts[1:]:
        gain = gain * one(*cut)
    return gain


def bell_draw(rng, dims, scale, most, shards=(), held_as=jnp.bfloat16):
    drawn = jax.random.normal(rng, dims, jnp.float32) * scale
    if len(shards) > 0:
        drawn = block_levels(rng, dims, shards, -0.22, 0.18) * drawn
    return jnp.clip(drawn, min=-most, max=most).astype(held_as)


def setup_inputs(seed: int = 0) -> dict:
    streams_of = jax.random.split(jax.random.key(seed), 6)
    hessian = draw_hessian(jax.random.fold_in(streams_of[5], 71), 0)
    weights = bell_draw(streams_of[1], (R, D), 1.0, 6.0, ((0, 8), (1, 4)))
    codes = touch_ends(jax.random.randint(streams_of[2], (R, D // 2), 0, CODES), jax.random.fold_in(streams_of[2], 1), 0, CODES - 1).astype(jnp.int32)
    tile_map = touch_ends(jax.random.randint(streams_of[3], (R // TILE_ROWS, D // TILE_COLS), 0, NB), jax.random.fold_in(streams_of[3], 1), 0, NB - 1).astype(jnp.int32)
    codebooks = bell_draw(streams_of[4], (NB, 2, CODES), 1.0, 6.0, (), jnp.float32)
    return {"hessian": hessian, "weights": weights, "codes": codes, "tile_map": tile_map, "codebooks": codebooks}


learn_rate = 0.01


def book_index(tile_map):
    spread = jnp.repeat(tile_map, TILE_ROWS, axis=0)
    return jnp.repeat(spread, TILE_COLS // 2, axis=1)


def reference(hessian, weights, codes, tile_map, codebooks):
    full_hessian = hessian.reshape(D, D)
    flat_index = (book_index(tile_map) * CODES + codes).astype(jnp.int32)
    for iteration in range(STEPS):
        table_even = codebooks[:, 0, :].reshape(-1)
        table_odd = codebooks[:, 1, :].reshape(-1)
        rebuilt = jnp.stack([table_even[flat_index], table_odd[flat_index]], axis=-1).reshape(R, D)
        error = rebuilt - weights.astype(jnp.float32)
        weight_grad = 2.0 * jnp.dot(error, full_hessian, precision=lax.Precision.HIGHEST)
        grad_even = jax.ops.segment_sum(weight_grad[:, 0::2].reshape(-1), flat_index.reshape(-1), NB * CODES)
        grad_odd = jax.ops.segment_sum(weight_grad[:, 1::2].reshape(-1), flat_index.reshape(-1), NB * CODES)
        book_grad = jnp.stack([grad_even.reshape(NB, CODES), grad_odd.reshape(NB, CODES)], axis=1)
        codebooks = codebooks - learn_rate * book_grad
    return codebooks
```

```python
import functools

import jax
import jax.numpy as jnp
from jax import lax
from jax.experimental import pallas as pl
from jax.experimental.pallas import tpu as pltpu
from jax.sharding import PartitionSpec as P

TILE_ROWS = 16
TILE_COLS = 256
STEPS = 2
LANES = 128
HALF = TILE_COLS // 2
CHUNK_TILES = 2
LOW = 32

learn_rate = 0.01
MESH = pl.DeviceIdType.MESH
NT = (((1,), (1,)), ((), ()))
VMEM = pl.BlockSpec(memory_space=pltpu.VMEM)
SMEM = pl.BlockSpec(memory_space=pltpu.SMEM)
ANY = pl.BlockSpec(memory_space=pl.ANY)
VMEM_BYTES = 62 * 2**20


def pick(table, index):
    return jnp.take_along_axis(table, index, axis=1, mode="promise_in_bounds")


def lookup(table, code):
    index = code & (LANES - 1)
    upper = code >= LANES
    tables = [jnp.broadcast_to(table[n : n + 1, :], code.shape) for n in range(4)]
    even = jnp.where(upper, pick(tables[2], index), pick(tables[0], index))
    odd = jnp.where(upper, pick(tables[3], index), pick(tables[1], index))
    return even, odd


def split_pairs(left, right):
    lane = lax.broadcasted_iota(jnp.int32, left.shape, 1)
    first = lane < LANES // 2
    index = (2 * lane) & (LANES - 1)
    even = jnp.where(first, pick(left, index), pick(right, index))
    odd = jnp.where(first, pick(left, index + 1), pick(right, index + 1))
    return even, odd


def halves(x):
    high = x.astype(jnp.bfloat16)
    return high, (x - high.astype(jnp.float32)).astype(jnp.bfloat16)


def three_products(a_high, a_low, b_high, b_low):
    dot = functools.partial(jnp.dot, preferred_element_type=jnp.float32)
    return dot(a_high, b_low) + dot(a_low, b_high) + dot(a_high, b_high)


def flip(chip, mask):
    bit = 0
    while mask >> bit:
        if (mask >> bit) & 1:
            size = 1 << bit
            chip = chip + (1 - 2 * lax.rem(chip // size, 2)) * size
        bit += 1
    return chip


def rows_of(index, size):
    return pl.ds(pl.multiple_of(index * size, size), size)


def first_kernel(n_col, chunks, map_ref, codes_ref, weights_ref, books_ref, hessian_ref, part_ref, high_out, low_out, errors, e_high, e_low, h_in, h_high, h_low, hop_send, hop_recv, pair_send, pair_recv, in_sem, high_sem, low_sem):
    r, c = lax.axis_index("row"), lax.axis_index("col")
    chip, core = c // 2, lax.rem(c, 2)
    chips = n_col // 2
    dims = chips.bit_length() - 1
    rows = codes_ref.shape[0]
    width = h_in.shape[3]
    pairs = CHUNK_TILES * HALF
    pair = (r, chip * 2 + 1 - core)

    barrier = pltpu.get_barrier_semaphore()
    for d in range(dims):
        pl.semaphore_signal(barrier, inc=1, device_id=(r, flip(chip, 1 << d) * 2 + core), device_id_type=MESH)
    pl.semaphore_signal(barrier, inc=1, device_id=pair, device_id_type=MESH)

    def fetch(k, slot):
        def one(n, carry):
            for parity in range(2):
                pltpu.make_async_copy(
                    hessian_ref.at[rows_of(k, pairs), parity, n, 0],
                    h_in.at[slot, parity, :, rows_of(n, LANES)],
                    in_sem.at[slot],
                ).start()
            return carry

        lax.fori_loop(0, width // LANES, one, 0)

    def out_copies(k, slot):
        return [
            pltpu.make_async_copy(h_high.at[slot], high_out.at[k], high_sem.at[slot]),
            pltpu.make_async_copy(h_low.at[slot], low_out.at[k], low_sem.at[slot]),
        ]

    fetch(0, 0)
    if chunks > 1:
        fetch(1, 1)

    def order(phase):
        return [(phase + i) % dims for i in range(dims)]

    def last(mask, phase):
        return max([i for i, d in enumerate(order(phase)) if (mask >> d) & 1], default=-1)

    def block(k, mask, which):
        return errors.at[k, rows_of(flip(chip, mask) * 2 + which, rows)]

    def hop(k, mask, dim):
        here = block(k, mask, core)
        target = mask | (1 << dim)
        return pltpu.make_async_remote_copy(
            src_ref=here,
            dst_ref=here,
            send_sem=hop_send.at[k, target],
            recv_sem=hop_recv.at[k, target],
            device_id=(r, flip(chip, 1 << dim) * 2 + core),
            device_id_type=MESH,
        )

    def across(k, mask):
        here = block(k, mask, core)
        return pltpu.make_async_remote_copy(
            src_ref=here,
            dst_ref=here,
            send_sem=pair_send.at[k, mask],
            recv_sem=pair_recv.at[k, mask],
            device_id=pair,
            device_id_type=MESH,
        )

    def arrival(k, mask, phase):
        dim = order(phase)[last(mask, phase)]
        here = block(k, mask, core)
        return pltpu.make_async_remote_copy(
            src_ref=here,
            dst_ref=here,
            send_sem=hop_send.at[k, mask],
            recv_sem=hop_recv.at[k, mask],
            device_id=(r, flip(chip, 1 << dim) * 2 + core),
            device_id_type=MESH,
        )

    def pair_arrival(k, mask):
        here = block(k, mask, 1 - core)
        return pltpu.make_async_remote_copy(
            src_ref=here,
            dst_ref=here,
            send_sem=pair_send.at[k, mask],
            recv_sem=pair_recv.at[k, mask],
            device_id=pair,
            device_id_type=MESH,
        )

    def pass_on(k, mask, phase):
        for i in range(last(mask, phase) + 1, dims):
            hop(k, mask, order(phase)[i]).start()
        across(k, mask).start()

    def own(k, phase):
        for t in range(CHUNK_TILES):
            for i in range(rows // TILE_ROWS):
                lines = pl.ds(i * TILE_ROWS, TILE_ROWS)
                j = k * CHUNK_TILES + t
                codes = codes_ref[lines, rows_of(j, HALF)]
                even, odd = lookup(books_ref[map_ref[i, j]], codes)
                left = weights_ref[lines, rows_of(2 * j, LANES)].astype(jnp.float32)
                right = weights_ref[lines, rows_of(2 * j + 1, LANES)].astype(jnp.float32)
                w_even, w_odd = split_pairs(left, right)
                place = pl.ds(pl.multiple_of(c * rows + i * TILE_ROWS, TILE_ROWS), TILE_ROWS)
                errors[k, place, t * HALF : (t + 1) * HALF] = even - w_even
                errors[k, place, pairs + t * HALF : pairs + (t + 1) * HALF] = odd - w_odd
        pass_on(k, 0, phase)

    def product(k):
        slot = lax.rem(k, 2)
        pltpu.make_async_copy(h_in.at[slot], h_in.at[slot], in_sem.at[slot]).wait()

        @pl.when(k >= 2)
        def _():
            for copy in out_copies(k - 2, slot):
                copy.wait()

        step = 64

        def convert(n, carry):
            for parity in range(2):
                high, low = halves(h_in[slot, parity, rows_of(n, step), :])
                place = pl.ds(pl.multiple_of(parity * pairs + n * step, step), step)
                h_high[slot, place, :] = high
                h_low[slot, place, :] = low
            return carry

        lax.fori_loop(0, pairs // step, convert, 0)
        for copy in out_copies(k, slot):
            copy.start()

        @pl.when(k + 2 < chunks)
        def _():
            fetch(k + 2, slot)

        def convert_error(n, carry):
            place = rows_of(n, step)
            high, low = halves(errors[k, place, :])
            e_high[place, :] = high
            e_low[place, :] = low
            return carry

        for mask in range(chips):
            pair_arrival(k, mask).wait_recv()
        lax.fori_loop(0, errors.shape[1] // step, convert_error, 0)
        total = three_products(e_high[...], e_low[...], h_high[slot], h_low[slot])

        @pl.when(k == 0)
        def _():
            part_ref[...] = total

        @pl.when(k > 0)
        def _():
            part_ref[...] += total

    pl.semaphore_wait(barrier, dims + 1)
    own(0, 0)

    def turn(step, carry):
        for u in range(dims):
            t = step * dims + u

            @pl.when(t + 1 < chunks)
            def _():
                own(t + 1, (u + 1) % dims)

            for level in range(1, dims + 1):
                k = t - level + 1
                phase = (u - level + 1) % dims

                @pl.when((k >= 0) & (k < chunks))
                def _():
                    for mask in range(1, chips):
                        if mask.bit_count() == level:
                            arrival(k, mask, phase).wait_recv()
                            pass_on(k, mask, phase)

            k = t - dims

            @pl.when((k >= 0) & (k < chunks))
            def _():
                product(k)

        return carry

    lax.fori_loop(0, -(-(chunks + dims) // dims), turn, 0)
    for k in range(max(0, chunks - 2), chunks):
        for copy in out_copies(k, k % 2):
            copy.wait()

    def drain(k, carry):
        for mask in range(chips):
            across(k, mask).wait_send()
            if mask:
                arrival(k, mask, 0).wait_send()
        return carry

    lax.fori_loop(0, chunks, drain, 0)


def first_product(n_col, tile_map, codes, weights, books, hessian):
    rows, length = weights.shape
    count = hessian.shape[0]
    width = hessian.shape[1] * hessian.shape[2] * hessian.shape[3]
    size = CHUNK_TILES * TILE_COLS
    chunks = count // size
    total_rows = rows * n_col
    chips = n_col // 2
    dma = pltpu.SemaphoreType.DMA
    whole = jax.ShapeDtypeStruct((chunks, size, width), jnp.bfloat16)
    return pl.pallas_call(
        functools.partial(first_kernel, n_col, chunks),
        in_specs=[SMEM, VMEM, VMEM, VMEM, ANY],
        out_specs=[VMEM, ANY, ANY],
        out_shape=[jax.ShapeDtypeStruct((total_rows, width), jnp.float32), whole, whole],
        scratch_shapes=[
            pltpu.VMEM((chunks, total_rows, size), jnp.float32),
            pltpu.VMEM((total_rows, size), jnp.bfloat16),
            pltpu.VMEM((total_rows, size), jnp.bfloat16),
            pltpu.VMEM((2, 2, size // 2, width), jnp.float32),
            pltpu.VMEM((2, size, width), jnp.bfloat16),
            pltpu.VMEM((2, size, width), jnp.bfloat16),
            dma((chunks, chips)),
            dma((chunks, chips)),
            dma((chunks, chips)),
            dma((chunks, chips)),
            dma((2,)),
            dma((2,)),
            dma((2,)),
        ],
        compiler_params=pltpu.CompilerParams(collective_id=1, has_side_effects=True, vmem_limit_bytes=VMEM_BYTES),
        cost_estimate=pl.CostEstimate(flops=6 * total_rows * width * count, bytes_accessed=8 * count * width, transcendentals=0),
        name="first_product",
    )(tile_map, codes, weights, books.reshape(-1, 4, LANES), hessian.reshape(count // 2, 2, width // LANES, 1, LANES))


def next_kernel(place_ref, map_ref, codes_ref, delta_ref, high_ref, low_ref, part_ref, d_high, d_low):
    k = pl.program_id(0)
    down = codes_ref.shape[0] // TILE_ROWS
    pairs = CHUNK_TILES * HALF
    begin = place_ref[0] + k * CHUNK_TILES

    def line(i, carry):
        lines = rows_of(i, TILE_ROWS)
        for t in range(CHUNK_TILES):
            codes = codes_ref[lines, t * HALF : (t + 1) * HALF]
            even, odd = lookup(delta_ref[map_ref[i, begin + t]], codes)
            for part, value in enumerate((even, odd)):
                high, low = halves(value)
                at = part * pairs + t * HALF
                d_high[lines, at : at + HALF] = high
                d_low[lines, at : at + HALF] = low
        return carry

    lax.fori_loop(0, down, line, 0, unroll=2)
    total = three_products(d_high[...], d_low[...], high_ref[0], low_ref[0])

    @pl.when(k == 0)
    def _():
        part_ref[...] = total

    @pl.when(k > 0)
    def _():
        part_ref[...] += total


def next_product(begin, full_map, codes, delta, high, low):
    chunks, size, width = high.shape
    m = codes.shape[0]
    spec = pl.BlockSpec((1, size, width), lambda k: (k, 0, 0))
    return pl.pallas_call(
        next_kernel,
        grid=(chunks,),
        in_specs=[
            SMEM,
            SMEM,
            pl.BlockSpec((m, size // 2), lambda k: (0, k)),
            pl.BlockSpec((delta.shape[0] // 4, 4, LANES), lambda k: (0, 0, 0)),
            spec,
            spec,
        ],
        out_specs=pl.BlockSpec((m, width), lambda k: (0, 0)),
        out_shape=jax.ShapeDtypeStruct((m, width), jnp.float32),
        scratch_shapes=[pltpu.VMEM((m, size), jnp.bfloat16), pltpu.VMEM((m, size), jnp.bfloat16)],
        compiler_params=pltpu.CompilerParams(vmem_limit_bytes=VMEM_BYTES),
        cost_estimate=pl.CostEstimate(flops=6 * m * width * size * chunks, bytes_accessed=4 * size * chunks * width, transcendentals=0),
        name="next_product",
    )(begin, full_map, codes, delta.reshape(-1, 4, LANES), high, low)


def spread_tile(codes, left, right):
    even, odd = split_pairs(left, right)
    values = []
    for x in (even, odd):
        high = x.astype(jnp.bfloat16).astype(jnp.float32)
        values += [high, x - high]
    upper = codes // LOW
    lower = (codes & (LOW - 1)).astype(jnp.float32).astype(jnp.bfloat16)
    eight = lax.broadcasted_iota(jnp.int32, (8, LANES), 0)
    entry = lax.broadcasted_iota(jnp.int32, (LOW, LANES), 0).astype(jnp.float32).astype(jnp.bfloat16)
    one, zero = jnp.bfloat16(1), jnp.bfloat16(0)
    parts, hots = [], []
    for n in range(TILE_ROWS):
        fits = eight == upper[n : n + 1, :]
        part = jnp.concatenate([jnp.where(fits, x[n : n + 1, :], 0.0) for x in values], axis=0)
        parts.append(part.astype(jnp.bfloat16))
        hots.append(jnp.where(entry == lower[n : n + 1, :], one, zero))
    return lax.dot_general(
        jnp.concatenate(parts, axis=1), jnp.concatenate(hots, axis=1), NT, preferred_element_type=jnp.float32
    )


def scatter_kernel(run, gap, place_ref, map_ref, codes_ref, grad_ref, books_ref, sums_ref):
    g = pl.program_id(0)
    rows_here, pairs = codes_ref.shape
    down, across = rows_here // TILE_ROWS, pairs // HALF
    top = g * down
    begin = place_ref[0]
    halves_apart = run % TILE_COLS != 0
    row = lax.broadcasted_iota(jnp.int32, (8, LOW), 0)
    lane = lax.broadcasted_iota(jnp.int32, (TILE_ROWS, LANES), 1)

    @pl.when(g == 0)
    def _():
        sums_ref[...] = jnp.zeros_like(sums_ref)

    def book(i, column):
        return map_ref[top + i, ((column // run) * gap + begin + column % run) // TILE_COLS]

    def add(index, sums):
        even, odd = sums[0:8] + sums[8:16], sums[16:24] + sums[24:32]
        first = jnp.where(row < 4, even, jnp.concatenate([odd[4:8], odd[0:4]], axis=0))
        second = jnp.where(row < 4, jnp.concatenate([even[4:8], even[0:4]], axis=0), odd)
        sums_ref[index, :, 0:LOW] += jnp.concatenate([first, second], axis=0)

    def tile(t, carry):
        i, j = t // across, t % across
        rows = rows_of(i, TILE_ROWS)
        codes = codes_ref[rows, rows_of(j, HALF)]
        left = grad_ref[rows, rows_of(2 * j, LANES)]
        right = grad_ref[rows, rows_of(2 * j + 1, LANES)]
        if halves_apart:
            none = jnp.zeros_like(left)
            add(book(i, j * TILE_COLS), spread_tile(codes, left, none))
            add(book(i, j * TILE_COLS + LANES), spread_tile(codes, none, right))
        else:
            add(book(i, j * TILE_COLS), spread_tile(codes, left, right))
        return carry

    lax.fori_loop(0, down * across, tile, 0, unroll=1 if halves_apart else 4)

    @pl.when(g == pl.num_programs(0) - 1)
    def _():
        count = sums_ref.shape[0]
        groups = LANES // LOW
        step = 16
        size = step * 4

        def squeeze(n, carry):
            x = sums_ref[rows_of(n, step)].reshape(size, groups, LANES)
            total = x[:, 0, :]
            for b in range(1, groups):
                total = total + pltpu.roll(x[:, b, :], b * LOW, 1)
            books_ref[rows_of(n, size), :] = total
            return carry

        lax.fori_loop(0, count // step, squeeze, 0)


def scatter(run, gap, begin, full_map, codes, grad, shape):
    m, n = grad.shape
    block = min(m, 128)
    return pl.pallas_call(
        functools.partial(scatter_kernel, run, gap),
        grid=(m // block,),
        in_specs=[
            SMEM,
            SMEM,
            pl.BlockSpec((block, n // 2), lambda i: (i, 0)),
            pl.BlockSpec((block, n), lambda i: (i, 0)),
        ],
        out_specs=pl.BlockSpec(shape, lambda i: (0, 0)),
        out_shape=jax.ShapeDtypeStruct(shape, jnp.float32),
        scratch_shapes=[pltpu.VMEM((shape[0] // 4, 16, LANES), jnp.float32)],
        compiler_params=pltpu.CompilerParams(vmem_limit_bytes=VMEM_BYTES),
        cost_estimate=pl.CostEstimate(flops=64 * 32 * m * n, bytes_accessed=6 * m * n, transcendentals=0),
        name="scatter",
    )(begin, full_map, codes, grad)


def update_kernel(n_row, n_col, final, grad_ref, books_ref, delta_ref, out_ref, pair_in, pair_sum, chip_in, chip_sum, row_in, *sems):
    r, c = lax.axis_index("row"), lax.axis_index("col")
    chip, core = c // 2, lax.rem(c, 2)
    chips = n_col // 2
    half = grad_ref.shape[0] // 2
    wide = half // chips
    thin = wide // n_row
    pair = (r, chip * 2 + 1 - core)
    others = [lax.rem(chip + d, chips) for d in range(chips)]
    lines = [lax.rem(r + d, n_row) for d in range(n_row)]

    barrier = pltpu.get_barrier_semaphore()
    pl.semaphore_signal(barrier, inc=1, device_id=pair, device_id_type=MESH)
    for d in range(1, chips):
        pl.semaphore_signal(barrier, inc=1, device_id=(r, others[d] * 2 + core), device_id_type=MESH)
    for d in range(1, n_row):
        pl.semaphore_signal(barrier, inc=1, device_id=(lines[d], c), device_id_type=MESH)
    pl.semaphore_wait(barrier, chips + n_row - 1)

    pair_send, pair_recv, chip_send, chip_recv, row_send, row_recv, row_send2, row_recv2, chip_send2, chip_recv2, pair_send2, pair_recv2 = sems

    def send(src, dst, sends, recvs, d, device):
        copy = pltpu.make_async_remote_copy(
            src_ref=src, dst_ref=dst, send_sem=sends.at[d], recv_sem=recvs.at[d], device_id=device, device_id_type=MESH
        )
        copy.start()
        return copy

    def total_of(first, received, copies):
        for d, copy in enumerate(copies, 1):
            copy.wait_recv()
            first = first + received[d]
        return first

    copies = []
    swap = send(grad_ref.at[rows_of(1 - core, half)], pair_in, pair_send, pair_recv, 0, pair)
    swap.wait_recv()
    pair_sum[...] = grad_ref[rows_of(core, half), :] + pair_in[...]
    first = [
        send(pair_sum.at[rows_of(others[d], wide)], chip_in.at[d], chip_send, chip_recv, d, (r, others[d] * 2 + core))
        for d in range(1, chips)
    ]
    chip_sum[...] = total_of(pair_sum[rows_of(chip, wide), :], chip_in, first)
    second = [
        send(chip_sum.at[rows_of(lines[d], thin)], row_in.at[d], row_send, row_recv, d, (lines[d], c))
        for d in range(1, n_row)
    ]
    total = total_of(chip_sum[rows_of(r, thin), :], row_in, second)
    mine = rows_of((core * chips + chip) * n_row + r, thin)
    change = -learn_rate * (2.0 * total)
    if final:
        out_ref[mine, :] = books_ref[mine, :] + (2.0 * delta_ref[mine, :] + change)
    else:
        out_ref[mine, :] = change
    third = [send(out_ref.at[mine], out_ref.at[mine], row_send2, row_recv2, d, (lines[d], c)) for d in range(1, n_row)]
    for copy in third:
        copy.wait_recv()
    piece = rows_of(core * chips + chip, wide)
    fourth = [
        send(out_ref.at[piece], out_ref.at[piece], chip_send2, chip_recv2, d, (r, others[d] * 2 + core))
        for d in range(1, chips)
    ]
    for copy in fourth:
        copy.wait_recv()
    part = rows_of(core, half)
    fifth = send(out_ref.at[part], out_ref.at[part], pair_send2, pair_recv2, 0, pair)
    fifth.wait_recv()
    for copy in [swap, fifth] + first + second + third + fourth:
        copy.wait_send()


def update(n_row, n_col, final, grad, books, delta):
    half = grad.shape[0] // 2
    chips = n_col // 2
    wide = half // chips
    thin = wide // n_row
    dma = pltpu.SemaphoreType.DMA
    sizes = [1, 1, chips, chips, n_row, n_row, n_row, n_row, chips, chips, 1, 1]
    return pl.pallas_call(
        functools.partial(update_kernel, n_row, n_col, final),
        in_specs=[VMEM, VMEM, VMEM],
        out_specs=VMEM,
        out_shape=jax.ShapeDtypeStruct(grad.shape, jnp.float32),
        scratch_shapes=[
            pltpu.VMEM((half, LANES), jnp.float32),
            pltpu.VMEM((half, LANES), jnp.float32),
            pltpu.VMEM((chips, wide, LANES), jnp.float32),
            pltpu.VMEM((wide, LANES), jnp.float32),
            pltpu.VMEM((n_row, thin, LANES), jnp.float32),
        ]
        + [dma((size,)) for size in sizes],
        compiler_params=pltpu.CompilerParams(collective_id=2 if final else 0, has_side_effects=True),
        name="last_update" if final else "update",
    )(grad, books, delta)


def per_device(n_row, n_col, hessian, weights, codes, tile_map, codebooks):
    count, parts, entries = codebooks.shape
    books = codebooks.reshape(count, parts, entries // LANES, LANES).transpose(0, 2, 1, 3).reshape(-1, LANES)
    run = hessian.shape[2] * hessian.shape[3]
    r, c = lax.axis_index("row"), lax.axis_index("col")
    begin_row = jnp.full((1,), r * tile_map.shape[1], jnp.int32)
    begin_col = jnp.full((1,), c * run, jnp.int32)

    full_map = lax.all_gather(lax.all_gather(tile_map, "row", axis=1, tiled=True), "col", axis=0, tiled=True)
    code_piece = lax.all_to_all(codes, "col", split_axis=1, concat_axis=0, tiled=True)
    code_spread = lax.all_gather(code_piece, "row", axis=1, tiled=True)

    grad, high, low = first_product(n_col, tile_map, codes, weights, books, hessian)
    grad, held_codes = lax.optimization_barrier((grad, codes))
    code_plane = lax.all_gather(held_codes, "col", axis=0, tiled=True)
    sums = scatter(run, n_col * run, begin_col, full_map, code_spread, grad, books.shape)
    delta = update(n_row, n_col, False, sums, books, books)
    grad = next_product(begin_row, full_map, code_plane, delta, high, low)
    sums = scatter(run, n_col * run, begin_col, full_map, code_spread, grad, books.shape)
    books = update(n_row, n_col, True, sums, books, delta)
    return books.reshape(count, entries // LANES, parts, LANES).transpose(0, 2, 1, 3).reshape(codebooks.shape)


def solution(mesh):
    placed = (P("row", None, "col", None), P("col", "row"), P("col", "row"), P("col", "row"), P())
    body = functools.partial(per_device, mesh.shape["row"], mesh.shape["col"])
    return jax.shard_map(body, mesh=mesh, in_specs=placed, out_specs=P(), check_vma=False)
```

```python
import functools

import jax
import jax.numpy as jnp
from jax import lax
from jax.experimental import pallas as pl
from jax.experimental.pallas import tpu as pltpu
from jax.sharding import PartitionSpec as P

TILE_ROWS = 16
TILE_COLS = 256
STEPS = 2
LANES = 128
HALF = TILE_COLS // 2
CHUNK_TILES = 2
LOW = 32

learn_rate = 0.01
MESH = pl.DeviceIdType.MESH
NT = (((1,), (1,)), ((), ()))
VMEM = pl.BlockSpec(memory_space=pltpu.VMEM)
SMEM = pl.BlockSpec(memory_space=pltpu.SMEM)
ANY = pl.BlockSpec(memory_space=pl.ANY)
VMEM_BYTES = 62 * 2**20


def pick(table, index):
    return jnp.take_along_axis(table, index, axis=1, mode="promise_in_bounds")


def lookup(table, code):
    index = code & (LANES - 1)
    upper = code >= LANES
    tables = [jnp.broadcast_to(table[n : n + 1, :], code.shape) for n in range(4)]
    even = jnp.where(upper, pick(tables[2], index), pick(tables[0], index))
    odd = jnp.where(upper, pick(tables[3], index), pick(tables[1], index))
    return even, odd


def split_pairs(left, right):
    lane = lax.broadcasted_iota(jnp.int32, left.shape, 1)
    first = lane < LANES // 2
    index = (2 * lane) & (LANES - 1)
    even = jnp.where(first, pick(left, index), pick(right, index))
    odd = jnp.where(first, pick(left, index + 1), pick(right, index + 1))
    return even, odd


def halves(x):
    high = x.astype(jnp.bfloat16)
    return high, (x - high.astype(jnp.float32)).astype(jnp.bfloat16)


def three_products(a_high, a_low, b_high, b_low):
    dot = functools.partial(jnp.dot, preferred_element_type=jnp.float32)
    return dot(a_high, b_low) + dot(a_low, b_high) + dot(a_high, b_high)


def flip(chip, mask):
    bit = 0
    while mask >> bit:
        if (mask >> bit) & 1:
            size = 1 << bit
            chip = chip + (1 - 2 * lax.rem(chip // size, 2)) * size
        bit += 1
    return chip


def rows_of(index, size):
    return pl.ds(pl.multiple_of(index * size, size), size)


class Cube:
    def __init__(self, n_col, view, first, sems):
        self.r, c = lax.axis_index("row"), lax.axis_index("col")
        self.chip, self.core = c // 2, lax.rem(c, 2)
        self.chips = n_col // 2
        self.dims = self.chips.bit_length() - 1
        self.view, self.first = view, first
        self.hop_send, self.hop_recv, self.pair_send, self.pair_recv = sems

    def order(self, phase):
        return [(phase + i) % self.dims for i in range(self.dims)]

    def last(self, mask, phase):
        return max([i for i, d in enumerate(self.order(phase)) if (mask >> d) & 1], default=-1)

    def block(self, k, mask, core):
        return self.view(k, flip(self.chip, mask) * 2 + core)

    def copy(self, k, mask, target, sends, recvs, device, core):
        here = self.block(k, mask, core)
        return pltpu.make_async_remote_copy(
            src_ref=here if mask or self.first is None else self.first(k),
            dst_ref=here,
            send_sem=sends.at[k, target],
            recv_sem=recvs.at[k, target],
            device_id=device,
            device_id_type=MESH,
        )

    def hop(self, k, mask, target, dim):
        device = (self.r, flip(self.chip, 1 << dim) * 2 + self.core)
        return self.copy(k, mask, target, self.hop_send, self.hop_recv, device, self.core)

    def across(self, k, mask):
        device = (self.r, self.chip * 2 + 1 - self.core)
        return self.copy(k, mask, mask, self.pair_send, self.pair_recv, device, self.core)

    def pass_on(self, k, mask, phase):
        for i in range(self.last(mask, phase) + 1, self.dims):
            dim = self.order(phase)[i]
            self.hop(k, mask, mask | (1 << dim), dim).start()
        self.across(k, mask).start()

    def arrivals(self, k, level, phase):
        for mask in range(1, self.chips):
            if mask.bit_count() == level:
                self.hop(k, mask, mask, self.order(phase)[self.last(mask, phase)]).wait_recv()
                self.pass_on(k, mask, phase)

    def pair_arrivals(self, k):
        device = (self.r, self.chip * 2 + 1 - self.core)
        for mask in range(self.chips):
            self.copy(k, mask, mask, self.pair_send, self.pair_recv, device, 1 - self.core).wait_recv()

    def drain(self, chunks):
        def one(k, carry):
            for mask in range(self.chips):
                self.across(k, mask).wait_send()
                if mask:
                    self.hop(k, mask, mask, 0).wait_send()
            return carry

        lax.fori_loop(0, chunks, one, 0)

    def turns(self, chunks, extra, begin, work):
        unroll = self.dims * (1 + self.dims % 2)
        count = chunks + self.dims + extra

        def turn(step, carry):
            for u in range(unroll):
                t = step * unroll + u

                @pl.when(t + 1 < chunks)
                def _():
                    begin(t + 1, u + 1)

                for level in range(1, self.dims + 1):
                    k = t - level + 1

                    @pl.when((k >= 0) & (k < chunks))
                    def _():
                        self.arrivals(k, level, (u - level + 1) % self.dims)

                work(t - self.dims, (u - self.dims) % 2)
            return carry

        lax.fori_loop(0, -(-count // unroll), turn, 0)


def greet(devices):
    barrier = pltpu.get_barrier_semaphore()
    for device in devices:
        pl.semaphore_signal(barrier, inc=1, device_id=device, device_id_type=MESH)
    pl.semaphore_wait(barrier, len(devices))


def first_kernel(n_row, n_col, chunks, run, map_ref, padded_ref, codes_ref, weights_ref, books_ref, hessian_ref, part_ref, high_out, low_out, spread_out, maps_out, errors, e_high, e_low, h_in, high0, high1, low0, low1, hop_send, hop_recv, pair_send, pair_recv, in_sem, out_sem, code_send, code_recv, own_sem, line_send, line_recv, map_send, map_recv, map_send2, map_recv2):
    r, c = lax.axis_index("row"), lax.axis_index("col")
    rows = codes_ref.shape[0]
    width = h_in.shape[3]
    pairs = CHUNK_TILES * HALF
    h_high, h_low = (high0, high1), (low0, low1)
    cols = [lax.rem(c + d, n_col) for d in range(n_col)]
    lines = [lax.rem(r + d, n_row) for d in range(n_row)]
    cube = Cube(n_col, lambda k, at: errors.at[k, rows_of(at, rows)], None, (hop_send, hop_recv, pair_send, pair_recv))

    def fetch(k, slot):
        def one(n, carry):
            for parity in range(2):
                pltpu.make_async_copy(
                    hessian_ref.at[rows_of(k, pairs), parity, n, 0],
                    h_in.at[slot, parity, :, rows_of(n, LANES)],
                    in_sem.at[slot],
                ).start()
            return carry

        lax.fori_loop(0, width // LANES, one, 0)

    def fetched(slot):
        pltpu.make_async_copy(h_in.at[slot], h_in.at[slot], in_sem.at[slot]).wait()

    def out_copies(k, slot):
        return [
            pltpu.make_async_copy(h_high[slot], high_out.at[k], out_sem.at[slot, 0]),
            pltpu.make_async_copy(h_low[slot], low_out.at[k], out_sem.at[slot, 1]),
        ]

    def convert(slot, columns):
        for parity in range(2):
            high, low = halves(h_in[slot, parity, :, columns])
            h_high[slot][parity * pairs : (parity + 1) * pairs, columns] = high
            h_low[slot][parity * pairs : (parity + 1) * pairs, columns] = low

    fetch(0, 0)
    if chunks > 1:
        fetch(1, 1)
    part_ref[...] = jnp.zeros_like(part_ref)
    maps_out[r, c] = padded_ref[...]
    greet([(r, cols[d]) for d in range(1, n_col)] + [(lines[d], c) for d in range(1, n_row)])

    span = max(run // 2, LANES)

    def piece(at):
        return codes_ref.at[:, rows_of(at * (run // 2) // span, span)]

    def send(src, dst, sends, recvs, d, device):
        return pltpu.make_async_remote_copy(
            src_ref=src, dst_ref=dst, send_sem=sends.at[d], recv_sem=recvs.at[d], device_id=device, device_id_type=MESH
        )

    here = spread_out.at[r, rows_of(c, rows)]
    spreads = [send(piece(cols[d]), here, code_send, code_recv, d, (r, cols[d])) for d in range(1, n_col)]
    maps = [send(padded_ref, maps_out.at[r, c], map_send, map_recv, d, (r, cols[d])) for d in range(1, n_col)]
    map_lines = [send(maps_out.at[r], maps_out.at[r], map_send2, map_recv2, d, (lines[d], c)) for d in range(1, n_row)]
    keep = pltpu.make_async_copy(piece(c), here, own_sem)

    def along(at, way):
        return pltpu.make_async_remote_copy(
            src_ref=spread_out.at[at],
            dst_ref=spread_out.at[at],
            send_sem=line_send.at[way, at],
            recv_sem=line_recv.at[way, at],
            device_id=(r + 1 - 2 * way, c),
            device_id_type=MESH,
        )

    def lines_start():
        for copy in maps + spreads:
            copy.wait_recv()
        keep.wait()
        for copy in map_lines:
            copy.start()

        @pl.when(r + 1 < n_row)
        def _():
            along(r, 0).start()

        @pl.when(r > 0)
        def _():
            along(r, 1).start()

    def lines_pass(d):
        @pl.when(r >= d)
        def _():
            along(r - d, 0).wait_recv()

            @pl.when(r + 1 < n_row)
            def _():
                along(r - d, 0).start()

        @pl.when(r + d < n_row)
        def _():
            along(r + d, 1).wait_recv()

            @pl.when(r > 0)
            def _():
                along(r + d, 1).start()

    def lines_drain():
        for copy in map_lines:
            copy.wait_recv()
        for copy in maps + spreads + map_lines:
            copy.wait_send()
        for d in range(n_row):
            @pl.when((r >= d) & (r + 1 < n_row))
            def _():
                along(r - d, 0).wait_send()

            @pl.when((r + d < n_row) & (r > 0))
            def _():
                along(r + d, 1).wait_send()

    def own(k, phase):
        for t in range(CHUNK_TILES):
            for i in range(rows // TILE_ROWS):
                at = pl.ds(i * TILE_ROWS, TILE_ROWS)
                j = k * CHUNK_TILES + t
                codes = codes_ref[at, rows_of(j, HALF)]
                even, odd = lookup(books_ref[map_ref[i, j]], codes)
                left = weights_ref[at, rows_of(2 * j, LANES)].astype(jnp.float32)
                right = weights_ref[at, rows_of(2 * j + 1, LANES)].astype(jnp.float32)
                w_even, w_odd = split_pairs(left, right)
                place = pl.ds(pl.multiple_of(c * rows + i * TILE_ROWS, TILE_ROWS), TILE_ROWS)
                errors[k, place, t * HALF : (t + 1) * HALF] = even - w_even
                errors[k, place, pairs + t * HALF : pairs + (t + 1) * HALF] = odd - w_odd
        cube.pass_on(k, 0, phase)

    nt = min(width, 512)

    def multiply(slot, columns):
        part_ref[:, columns] += three_products(e_high[...], e_low[...], h_high[slot][:, columns], h_low[slot][:, columns])

    def product(k, slot):
        step = 64

        @pl.when((k >= 0) & (k < chunks))
        def _():
            cube.pair_arrivals(k)

            def convert_error(n, carry):
                place = rows_of(n, step)
                e_high[place, :], e_low[place, :] = halves(errors[k, place, :])
                return carry

            lax.fori_loop(0, errors.shape[1] // step, convert_error, 0)

        @pl.when((k >= 0) & (k + 1 < chunks))
        def _():
            fetched(1 - slot)

            @pl.when(k >= 1)
            def _():
                for copy in out_copies(k - 1, 1 - slot):
                    copy.wait()

            def both(n, carry):
                columns = rows_of(n, nt)
                multiply(slot, columns)
                convert(1 - slot, columns)
                return carry

            lax.fori_loop(0, width // nt, both, 0)
            for copy in out_copies(k + 1, 1 - slot):
                copy.start()

            @pl.when(k + 3 < chunks)
            def _():
                fetch(k + 3, 1 - slot)

        @pl.when(k + 1 == chunks)
        def _():
            def alone(n, carry):
                multiply(slot, rows_of(n, nt))
                return carry

            lax.fori_loop(0, width // nt, alone, 0)

        @pl.when(k == 0)
        def _():
            lines_start()

        for d in range(1, n_row):
            @pl.when(k == min(2 * d, chunks - 1))
            def _():
                lines_pass(d)

    for copy in spreads + maps + [keep]:
        copy.start()
    own(0, 0)
    fetched(0)

    def convert_first(n, carry):
        convert(0, rows_of(n, nt))
        return carry

    lax.fori_loop(0, width // nt, convert_first, 0)
    for copy in out_copies(0, 0):
        copy.start()
    if chunks > 2:
        fetch(2, 0)

    cube.turns(chunks, 0, own, product)
    for k in range(max(0, chunks - 2), chunks):
        for copy in out_copies(k, k % 2):
            copy.wait()
    lines_drain()
    cube.drain(chunks)


def first_product(n_row, n_col, tile_map, padded, codes, weights, books, hessian):
    rows, length = weights.shape
    count = hessian.shape[0]
    run = hessian.shape[2] * hessian.shape[3]
    width = hessian.shape[1] * run
    size = CHUNK_TILES * TILE_COLS
    chunks = count // size
    total_rows = rows * n_col
    chips = n_col // 2
    dma = pltpu.SemaphoreType.DMA
    whole = jax.ShapeDtypeStruct((chunks, size, width), jnp.bfloat16)
    block = pltpu.VMEM((size, width), jnp.bfloat16)
    return pl.pallas_call(
        functools.partial(first_kernel, n_row, n_col, chunks, run),
        in_specs=[SMEM, VMEM, VMEM, VMEM, VMEM, ANY],
        out_specs=[VMEM, ANY, ANY, ANY, VMEM],
        out_shape=[
            jax.ShapeDtypeStruct((total_rows, width), jnp.float32),
            whole,
            whole,
            jax.ShapeDtypeStruct((n_row, total_rows, max(run // 2, LANES)), jnp.int32),
            jax.ShapeDtypeStruct((n_row, n_col) + padded.shape, jnp.int32),
        ],
        scratch_shapes=[
            pltpu.VMEM((chunks, total_rows, size), jnp.float32),
            pltpu.VMEM((total_rows, size), jnp.bfloat16),
            pltpu.VMEM((total_rows, size), jnp.bfloat16),
            pltpu.VMEM((2, 2, size // 2, width), jnp.float32),
            block,
            block,
            block,
            block,
            dma((chunks, chips)),
            dma((chunks, chips)),
            dma((chunks, chips)),
            dma((chunks, chips)),
            dma((2,)),
            dma((2, 2)),
            dma((n_col,)),
            dma((n_col,)),
            dma,
            dma((2, n_row)),
            dma((2, n_row)),
            dma((n_col,)),
            dma((n_col,)),
            dma((n_row,)),
            dma((n_row,)),
        ],
        compiler_params=pltpu.CompilerParams(collective_id=1, has_side_effects=True, vmem_limit_bytes=VMEM_BYTES),
        cost_estimate=pl.CostEstimate(flops=6 * total_rows * width * count, bytes_accessed=8 * count * width, transcendentals=0),
        name="first_product",
    )(tile_map, padded, codes, weights, books.reshape(-1, 4, LANES), hessian.reshape(count // 2, 2, width // LANES, 1, LANES))


def next_kernel(n_col, chunks, down, map_ref, codes_ref, delta_ref, high_ref, low_ref, part_ref, codes_all, high0, high1, low0, low1, d_high0, d_high1, d_low0, d_low1, hop_send, hop_recv, pair_send, pair_recv, in_sem):
    r, c = lax.axis_index("row"), lax.axis_index("col")
    rows = codes_ref.shape[0]
    total_rows, width = part_ref.shape
    pairs = CHUNK_TILES * HALF
    h_high, h_low = (high0, high1), (low0, low1)
    d_high, d_low = (d_high0, d_high1), (d_low0, d_low1)
    cube = Cube(
        n_col,
        lambda k, at: codes_all.at[k, rows_of(at, rows)],
        lambda k: codes_ref.at[:, rows_of(k, pairs)],
        (hop_send, hop_recv, pair_send, pair_recv),
    )

    def fetch(k, slot):
        return [
            pltpu.make_async_copy(high_ref.at[k], h_high[slot], in_sem.at[slot, 0]),
            pltpu.make_async_copy(low_ref.at[k], h_low[slot], in_sem.at[slot, 1]),
        ]

    for k in range(min(2, chunks)):
        for copy in fetch(k, k):
            copy.start()
    part_ref[...] = jnp.zeros_like(part_ref)
    greet(
        [(r, flip(cube.chip, 1 << d) * 2 + cube.core) for d in range(cube.dims)] + [(r, cube.chip * 2 + 1 - cube.core)]
    )

    def own(k, phase):
        cube.pass_on(k, 0, phase)
        codes_all[k, rows_of(c, rows), :] = codes_ref[:, rows_of(k, pairs)]

    nt = min(width, 512)
    tiles = total_rows // TILE_ROWS
    share = tiles // (width // nt)

    def look(k, slot, n):
        for q in range(share):
            i = n * share + q
            at = rows_of(i, TILE_ROWS)
            for t in range(CHUNK_TILES):
                codes = codes_all[k, at, t * HALF : (t + 1) * HALF]
                book = map_ref[r, i // down, lax.rem(i, down), k * CHUNK_TILES + t]
                for part, value in enumerate(lookup(delta_ref[book], codes)):
                    high, low = halves(value)
                    left = part * pairs + t * HALF
                    d_high[slot][at, left : left + HALF] = high
                    d_low[slot][at, left : left + HALF] = low

    def multiply(slot, n):
        columns = rows_of(n, nt)
        part_ref[:, columns] += three_products(
            d_high[slot][...], d_low[slot][...], h_high[slot][:, columns], h_low[slot][:, columns]
        )

    def loop(body):
        def one(n, carry):
            body(n)
            return carry

        lax.fori_loop(0, width // nt, one, 0)

    def work(k, slot):
        @pl.when((k >= 0) & (k < chunks))
        def _():
            cube.pair_arrivals(k)

        @pl.when((k >= 1) & (k <= chunks))
        def _():
            for copy in fetch(k - 1, 1 - slot):
                copy.wait()

        @pl.when(k == 0)
        def _():
            loop(lambda n: look(k, slot, n))

        @pl.when((k >= 1) & (k < chunks))
        def _():
            def body(n):
                multiply(1 - slot, n)
                look(k, slot, n)

            loop(body)

        @pl.when(k == chunks)
        def _():
            loop(lambda n: multiply(1 - slot, n))

        @pl.when((k >= 1) & (k + 1 < chunks))
        def _():
            for copy in fetch(k + 1, 1 - slot):
                copy.start()

    own(0, 0)
    cube.turns(chunks, 1, own, work)
    cube.drain(chunks)


def next_product(n_col, down, maps, codes, delta, high, low):
    chunks, size, width = high.shape
    rows = codes.shape[0]
    m = rows * n_col
    chips = n_col // 2
    dma = pltpu.SemaphoreType.DMA
    block = pltpu.VMEM((size, width), jnp.bfloat16)
    factor = pltpu.VMEM((m, size), jnp.bfloat16)
    return pl.pallas_call(
        functools.partial(next_kernel, n_col, chunks, down),
        in_specs=[SMEM, VMEM, VMEM, ANY, ANY],
        out_specs=VMEM,
        out_shape=jax.ShapeDtypeStruct((m, width), jnp.float32),
        scratch_shapes=[pltpu.VMEM((chunks, m, size // 2), jnp.int32)]
        + [block] * 4
        + [factor] * 4
        + [dma((chunks, chips))] * 4
        + [dma((2, 2))],
        compiler_params=pltpu.CompilerParams(collective_id=3, has_side_effects=True, vmem_limit_bytes=VMEM_BYTES),
        cost_estimate=pl.CostEstimate(flops=6 * m * width * size * chunks, bytes_accessed=4 * size * chunks * width, transcendentals=0),
        name="next_product",
    )(maps, codes, delta.reshape(-1, 4, LANES), high, low)


def spread_tile(codes, left, right):
    even, odd = split_pairs(left, right)
    values = []
    for x in (even, odd):
        high = x.astype(jnp.bfloat16).astype(jnp.float32)
        values += [high, x - high]
    upper = codes // LOW
    lower = (codes & (LOW - 1)).astype(jnp.float32).astype(jnp.bfloat16)
    eight = lax.broadcasted_iota(jnp.int32, (8, LANES), 0)
    entry = lax.broadcasted_iota(jnp.int32, (LOW, LANES), 0).astype(jnp.float32).astype(jnp.bfloat16)
    one, zero = jnp.bfloat16(1), jnp.bfloat16(0)
    parts, hots = [], []
    for n in range(TILE_ROWS):
        fits = eight == upper[n : n + 1, :]
        part = jnp.concatenate([jnp.where(fits, x[n : n + 1, :], 0.0) for x in values], axis=0)
        parts.append(part.astype(jnp.bfloat16))
        hots.append(jnp.where(entry == lower[n : n + 1, :], one, zero))
    return lax.dot_general(
        jnp.concatenate(parts, axis=1), jnp.concatenate(hots, axis=1), NT, preferred_element_type=jnp.float32
    )


def scatter_kernel(run, gap, sizes, place_ref, map_ref, codes_ref, grad_ref, books_ref, sums_ref):
    g = pl.program_id(0)
    groups, rows_here, span = codes_ref.shape
    down, across = rows_here // TILE_ROWS, groups * span // HALF
    map_down, map_across = sizes
    top = g * down
    begin = place_ref[0]
    halves_apart = run % TILE_COLS != 0
    row = lax.broadcasted_iota(jnp.int32, (8, LOW), 0)

    @pl.when(g == 0)
    def _():
        sums_ref[...] = jnp.zeros_like(sums_ref)

    def book(i, column):
        line = top + i
        tile = ((column // run) * gap + begin + column % run) // TILE_COLS
        return map_ref[tile // map_across, line // map_down, line % map_down, tile % map_across]

    def add(index, sums):
        even, odd = sums[0:8] + sums[8:16], sums[16:24] + sums[24:32]
        first = jnp.where(row < 4, even, jnp.concatenate([odd[4:8], odd[0:4]], axis=0))
        second = jnp.where(row < 4, jnp.concatenate([even[4:8], even[0:4]], axis=0), odd)
        sums_ref[index, :, 0:LOW] += jnp.concatenate([first, second], axis=0)

    def tile(t, carry):
        i, j = t // across, t % across
        rows = rows_of(i, TILE_ROWS)
        codes = codes_ref[j // (span // HALF), rows, rows_of(j % (span // HALF), HALF)]
        left = grad_ref[rows, rows_of(2 * j, LANES)]
        right = grad_ref[rows, rows_of(2 * j + 1, LANES)]
        if halves_apart:
            none = jnp.zeros_like(left)
            add(book(i, j * TILE_COLS), spread_tile(codes, left, none))
            add(book(i, j * TILE_COLS + LANES), spread_tile(codes, none, right))
        else:
            add(book(i, j * TILE_COLS), spread_tile(codes, left, right))
        return carry

    lax.fori_loop(0, down * across, tile, 0, unroll=1 if halves_apart else 4)

    @pl.when(g == pl.num_programs(0) - 1)
    def _():
        count = sums_ref.shape[0]
        groups = LANES // LOW
        step = 16
        size = step * 4

        def squeeze(n, carry):
            x = sums_ref[rows_of(n, step)].reshape(size, groups, LANES)
            total = x[:, 0, :]
            for b in range(1, groups):
                total = total + pltpu.roll(x[:, b, :], b * LOW, 1)
            books_ref[rows_of(n, size), :] = total
            return carry

        lax.fori_loop(0, count // step, squeeze, 0)


def scatter(run, gap, sizes, begin, maps, codes, grad, shape):
    m, n = grad.shape
    block = min(m, 128)
    return pl.pallas_call(
        functools.partial(scatter_kernel, run, gap, sizes),
        grid=(m // block,),
        in_specs=[
            SMEM,
            SMEM,
            pl.BlockSpec((codes.shape[0], block, codes.shape[2]), lambda i: (0, i, 0)),
            pl.BlockSpec((block, n), lambda i: (i, 0)),
        ],
        out_specs=pl.BlockSpec(shape, lambda i: (0, 0)),
        out_shape=jax.ShapeDtypeStruct(shape, jnp.float32),
        scratch_shapes=[pltpu.VMEM((shape[0] // 4, 16, LANES), jnp.float32)],
        compiler_params=pltpu.CompilerParams(vmem_limit_bytes=VMEM_BYTES),
        cost_estimate=pl.CostEstimate(flops=64 * 32 * m * n, bytes_accessed=6 * m * n, transcendentals=0),
        name="scatter",
    )(begin, maps, codes, grad)


def update_kernel(n_row, n_col, final, grad_ref, books_ref, delta_ref, out_ref, pair_in, pair_sum, chip_in, chip_sum, row_in, *sems):
    r, c = lax.axis_index("row"), lax.axis_index("col")
    chip, core = c // 2, lax.rem(c, 2)
    chips = n_col // 2
    half = grad_ref.shape[0] // 2
    wide = half // chips
    thin = wide // n_row
    pair = (r, chip * 2 + 1 - core)
    others = [lax.rem(chip + d, chips) for d in range(chips)]
    lines = [lax.rem(r + d, n_row) for d in range(n_row)]

    barrier = pltpu.get_barrier_semaphore()
    pl.semaphore_signal(barrier, inc=1, device_id=pair, device_id_type=MESH)
    for d in range(1, chips):
        pl.semaphore_signal(barrier, inc=1, device_id=(r, others[d] * 2 + core), device_id_type=MESH)
    for d in range(1, n_row):
        pl.semaphore_signal(barrier, inc=1, device_id=(lines[d], c), device_id_type=MESH)
    pl.semaphore_wait(barrier, chips + n_row - 1)

    pair_send, pair_recv, chip_send, chip_recv, row_send, row_recv, row_send2, row_recv2, chip_send2, chip_recv2, pair_send2, pair_recv2 = sems

    def send(src, dst, sends, recvs, d, device):
        copy = pltpu.make_async_remote_copy(
            src_ref=src, dst_ref=dst, send_sem=sends.at[d], recv_sem=recvs.at[d], device_id=device, device_id_type=MESH
        )
        copy.start()
        return copy

    def total_of(first, received, copies):
        for d, copy in enumerate(copies, 1):
            copy.wait_recv()
            first = first + received[d]
        return first

    copies = []
    swap = send(grad_ref.at[rows_of(1 - core, half)], pair_in, pair_send, pair_recv, 0, pair)
    swap.wait_recv()
    pair_sum[...] = grad_ref[rows_of(core, half), :] + pair_in[...]
    first = [
        send(pair_sum.at[rows_of(others[d], wide)], chip_in.at[d], chip_send, chip_recv, d, (r, others[d] * 2 + core))
        for d in range(1, chips)
    ]
    chip_sum[...] = total_of(pair_sum[rows_of(chip, wide), :], chip_in, first)
    second = [
        send(chip_sum.at[rows_of(lines[d], thin)], row_in.at[d], row_send, row_recv, d, (lines[d], c))
        for d in range(1, n_row)
    ]
    total = total_of(chip_sum[rows_of(r, thin), :], row_in, second)
    mine = rows_of((core * chips + chip) * n_row + r, thin)
    change = -learn_rate * (2.0 * total)
    if final:
        out_ref[mine, :] = books_ref[mine, :] + (2.0 * delta_ref[mine, :] + change)
    else:
        out_ref[mine, :] = change
    third = [send(out_ref.at[mine], out_ref.at[mine], row_send2, row_recv2, d, (lines[d], c)) for d in range(1, n_row)]
    for copy in third:
        copy.wait_recv()
    piece = rows_of(core * chips + chip, wide)
    fourth = [
        send(out_ref.at[piece], out_ref.at[piece], chip_send2, chip_recv2, d, (r, others[d] * 2 + core))
        for d in range(1, chips)
    ]
    for copy in fourth:
        copy.wait_recv()
    part = rows_of(core, half)
    fifth = send(out_ref.at[part], out_ref.at[part], pair_send2, pair_recv2, 0, pair)
    fifth.wait_recv()
    for copy in [swap, fifth] + first + second + third + fourth:
        copy.wait_send()


def update(n_row, n_col, final, grad, books, delta):
    half = grad.shape[0] // 2
    chips = n_col // 2
    wide = half // chips
    thin = wide // n_row
    dma = pltpu.SemaphoreType.DMA
    sizes = [1, 1, chips, chips, n_row, n_row, n_row, n_row, chips, chips, 1, 1]
    return pl.pallas_call(
        functools.partial(update_kernel, n_row, n_col, final),
        in_specs=[VMEM, VMEM, VMEM],
        out_specs=VMEM,
        out_shape=jax.ShapeDtypeStruct(grad.shape, jnp.float32),
        scratch_shapes=[
            pltpu.VMEM((half, LANES), jnp.float32),
            pltpu.VMEM((half, LANES), jnp.float32),
            pltpu.VMEM((chips, wide, LANES), jnp.float32),
            pltpu.VMEM((wide, LANES), jnp.float32),
            pltpu.VMEM((n_row, thin, LANES), jnp.float32),
        ]
        + [dma((size,)) for size in sizes],
        compiler_params=pltpu.CompilerParams(collective_id=2 if final else 0, has_side_effects=True),
        name="last_update" if final else "update",
    )(grad, books, delta)


def per_device(n_row, n_col, hessian, weights, codes, tile_map, codebooks):
    count, parts, entries = codebooks.shape
    books = codebooks.reshape(count, parts, entries // LANES, LANES).transpose(0, 2, 1, 3).reshape(-1, LANES)
    run = hessian.shape[2] * hessian.shape[3]
    c = lax.axis_index("col")
    begin = jnp.full((1,), c * run, jnp.int32)
    down, across = tile_map.shape
    padded = jnp.pad(tile_map, ((0, -down % 8), (0, -across % LANES)))

    grad, high, low, spread, maps = first_product(n_row, n_col, tile_map, padded, codes, weights, books, hessian)
    if run // 2 < spread.shape[2]:
        groups, m, span = spread.shape
        spread = lax.dynamic_slice(spread, (0, 0, lax.rem(c * (run // 2), span)), (groups, m, run // 2))
        spread = spread.transpose(1, 0, 2).reshape(1, m, groups * (run // 2))
    split = functools.partial(scatter, run, n_col * run, (down, across), begin, maps, spread)
    delta = update(n_row, n_col, False, split(grad, books.shape), books, books)
    grad = next_product(n_col, down, maps, codes, delta, high, low)
    books = update(n_row, n_col, True, split(grad, books.shape), books, delta)
    return books.reshape(count, entries // LANES, parts, LANES).transpose(0, 2, 1, 3).reshape(codebooks.shape)


def solution(mesh):
    placed = (P("row", None, "col", None), P("col", "row"), P("col", "row"), P("col", "row"), P())
    body = functools.partial(per_device, mesh.shape["row"], mesh.shape["col"])
    return jax.shard_map(body, mesh=mesh, in_specs=placed, out_specs=P(), check_vma=False)
```

```python
import functools

import jax
import jax.numpy as jnp
from jax import lax
from jax.experimental import pallas as pl
from jax.experimental.pallas import tpu as pltpu
from jax.sharding import PartitionSpec as P

TILE_ROWS = 16
TILE_COLS = 256
STEPS = 2
LANES = 128
HALF = TILE_COLS // 2
CHUNK_TILES = 2
LOW = 32
PARTS = 2

learn_rate = 0.01
MESH = pl.DeviceIdType.MESH
NT = (((1,), (1,)), ((), ()))
VMEM = pl.BlockSpec(memory_space=pltpu.VMEM)
SMEM = pl.BlockSpec(memory_space=pltpu.SMEM)
ANY = pl.BlockSpec(memory_space=pl.ANY)
VMEM_BYTES = 62 * 2**20


def pick(table, index):
    return jnp.take_along_axis(table, index, axis=1, mode="promise_in_bounds")


def lookup(table, code):
    index = code & (LANES - 1)
    upper = code >= LANES
    tables = [jnp.broadcast_to(table[n : n + 1, :], code.shape) for n in range(4)]
    even = jnp.where(upper, pick(tables[2], index), pick(tables[0], index))
    odd = jnp.where(upper, pick(tables[3], index), pick(tables[1], index))
    return even, odd


def split_pairs(left, right):
    lane = lax.broadcasted_iota(jnp.int32, left.shape, 1)
    first = lane < LANES // 2
    index = (2 * lane) & (LANES - 1)
    even = jnp.where(first, pick(left, index), pick(right, index))
    odd = jnp.where(first, pick(left, index + 1), pick(right, index + 1))
    return even, odd


def halves(x):
    high = x.astype(jnp.bfloat16)
    return high, (x - high.astype(jnp.float32)).astype(jnp.bfloat16)


def three_products(a_high, a_low, b_high, b_low):
    dot = functools.partial(jnp.dot, preferred_element_type=jnp.float32)
    return dot(a_high, b_low) + dot(a_low, b_high) + dot(a_high, b_high)


def flip(chip, mask):
    bit = 0
    while mask >> bit:
        if (mask >> bit) & 1:
            size = 1 << bit
            chip = chip + (1 - 2 * lax.rem(chip // size, 2)) * size
        bit += 1
    return chip


def rows_of(index, size):
    return pl.ds(pl.multiple_of(index * size, size), size)


class Cube:
    def __init__(self, n_col, view, first, sems):
        self.r, c = lax.axis_index("row"), lax.axis_index("col")
        self.chip, self.core = c // 2, lax.rem(c, 2)
        self.chips = n_col // 2
        self.dims = self.chips.bit_length() - 1
        self.view, self.first = view, first
        self.hop_send, self.hop_recv, self.pair_send, self.pair_recv = sems

    def order(self, phase):
        return [(phase + i) % self.dims for i in range(self.dims)]

    def last(self, mask, phase):
        return max([i for i, d in enumerate(self.order(phase)) if (mask >> d) & 1], default=-1)

    def block(self, k, mask, core):
        return self.view(k, flip(self.chip, mask) * 2 + core)

    def copy(self, k, mask, target, sends, recvs, device, core):
        here = self.block(k, mask, core)
        return pltpu.make_async_remote_copy(
            src_ref=here if mask or self.first is None else self.first(k),
            dst_ref=here,
            send_sem=sends.at[k, target],
            recv_sem=recvs.at[k, target],
            device_id=device,
            device_id_type=MESH,
        )

    def hop(self, k, mask, target, dim):
        device = (self.r, flip(self.chip, 1 << dim) * 2 + self.core)
        return self.copy(k, mask, target, self.hop_send, self.hop_recv, device, self.core)

    def across(self, k, mask):
        device = (self.r, self.chip * 2 + 1 - self.core)
        return self.copy(k, mask, mask, self.pair_send, self.pair_recv, device, self.core)

    def pass_on(self, k, mask, phase):
        for i in range(self.last(mask, phase) + 1, self.dims):
            dim = self.order(phase)[i]
            self.hop(k, mask, mask | (1 << dim), dim).start()
        self.across(k, mask).start()

    def arrivals(self, k, level, phase):
        for mask in range(1, self.chips):
            if mask.bit_count() == level:
                self.hop(k, mask, mask, self.order(phase)[self.last(mask, phase)]).wait_recv()
                self.pass_on(k, mask, phase)

    def pair_arrivals(self, k):
        device = (self.r, self.chip * 2 + 1 - self.core)
        for mask in range(self.chips):
            self.copy(k, mask, mask, self.pair_send, self.pair_recv, device, 1 - self.core).wait_recv()

    def drain(self, chunks):
        def one(k, carry):
            for mask in range(self.chips):
                self.across(k, mask).wait_send()
                if mask:
                    self.hop(k, mask, mask, 0).wait_send()
            return carry

        lax.fori_loop(0, chunks, one, 0)

    def turns(self, chunks, extra, ahead, begin, work, prepare=lambda: None):
        unroll = self.dims * (1 + self.dims % 2)
        count = chunks + self.dims + extra
        for k in range(min(ahead, chunks)):
            begin(k, k)
        prepare()

        def turn(step, carry):
            for u in range(unroll):
                t = step * unroll + u

                for level in range(self.dims, 0, -1):
                    k = t - level + 1

                    @pl.when((k >= 0) & (k < chunks))
                    def _():
                        self.arrivals(k, level, (u - level + 1) % self.dims)

                @pl.when(t + ahead < chunks)
                def _():
                    begin(t + ahead, u + ahead)

                work(t - self.dims, (u - self.dims) % 2)
            return carry

        lax.fori_loop(0, -(-count // unroll), turn, 0)


def greet(devices):
    barrier = pltpu.get_barrier_semaphore()
    for device in devices:
        pl.semaphore_signal(barrier, inc=1, device_id=device, device_id_type=MESH)
    pl.semaphore_wait(barrier, len(devices))


def first_kernel(n_row, n_col, chunks, run, map_ref, padded_ref, codes_ref, weights_ref, books_ref, hessian_ref, part_ref, high_out, low_out, spread_out, maps_out, errors, e_high, e_low, h_in, high0, high1, low0, low1, hop_send, hop_recv, pair_send, pair_recv, in_sem, out_sem, code_send, code_recv, own_sem, line_send, line_recv, map_send, map_recv, map_send2, map_recv2):
    r, c = lax.axis_index("row"), lax.axis_index("col")
    rows = codes_ref.shape[0]
    width = h_in.shape[3]
    pairs = CHUNK_TILES * HALF
    h_high, h_low = (high0, high1), (low0, low1)
    cols = [lax.rem(c + d, n_col) for d in range(n_col)]
    lines = [lax.rem(r + d, n_row) for d in range(n_row)]
    cube = Cube(n_col, lambda k, at: errors.at[k, rows_of(at, rows)], None, (hop_send, hop_recv, pair_send, pair_recv))

    def fetch(k, slot):
        def one(n, carry):
            for parity in range(2):
                pltpu.make_async_copy(
                    hessian_ref.at[rows_of(k, pairs), parity, n, 0],
                    h_in.at[slot, parity, :, rows_of(n, LANES)],
                    in_sem.at[slot],
                ).start()
            return carry

        lax.fori_loop(0, width // LANES, one, 0)

    def fetched(slot):
        pltpu.make_async_copy(h_in.at[slot], h_in.at[slot], in_sem.at[slot]).wait()

    def out_copies(k, slot):
        return [
            pltpu.make_async_copy(h_high[slot], high_out.at[k], out_sem.at[slot, 0]),
            pltpu.make_async_copy(h_low[slot], low_out.at[k], out_sem.at[slot, 1]),
        ]

    def convert(slot, columns):
        for parity in range(2):
            high, low = halves(h_in[slot, parity, :, columns])
            h_high[slot][parity * pairs : (parity + 1) * pairs, columns] = high
            h_low[slot][parity * pairs : (parity + 1) * pairs, columns] = low

    fetch(0, 0)
    if chunks > 1:
        fetch(1, 1)
    part_ref[...] = jnp.zeros_like(part_ref)
    maps_out[r, c] = padded_ref[...]
    greet([(r, cols[d]) for d in range(1, n_col)] + [(lines[d], c) for d in range(1, n_row)])

    span = max(run // 2, LANES)

    def piece(at):
        return codes_ref.at[:, rows_of(at * (run // 2) // span, span)]

    def send(src, dst, sends, recvs, d, device):
        return pltpu.make_async_remote_copy(
            src_ref=src, dst_ref=dst, send_sem=sends.at[d], recv_sem=recvs.at[d], device_id=device, device_id_type=MESH
        )

    here = spread_out.at[r, rows_of(c, rows)]
    spreads = [send(piece(cols[d]), here, code_send, code_recv, d, (r, cols[d])) for d in range(1, n_col)]
    maps = [send(padded_ref, maps_out.at[r, c], map_send, map_recv, d, (r, cols[d])) for d in range(1, n_col)]
    map_lines = [send(maps_out.at[r], maps_out.at[r], map_send2, map_recv2, d, (lines[d], c)) for d in range(1, n_row)]
    keep = pltpu.make_async_copy(piece(c), here, own_sem)

    def along(at, way):
        return pltpu.make_async_remote_copy(
            src_ref=spread_out.at[at],
            dst_ref=spread_out.at[at],
            send_sem=line_send.at[way, at],
            recv_sem=line_recv.at[way, at],
            device_id=(r + 1 - 2 * way, c),
            device_id_type=MESH,
        )

    def lines_start():
        for copy in maps + spreads:
            copy.wait_recv()
        keep.wait()
        for copy in map_lines:
            copy.start()

        @pl.when(r + 1 < n_row)
        def _():
            along(r, 0).start()

        @pl.when(r > 0)
        def _():
            along(r, 1).start()

    def lines_pass(d):
        @pl.when(r >= d)
        def _():
            along(r - d, 0).wait_recv()

            @pl.when(r + 1 < n_row)
            def _():
                along(r - d, 0).start()

        @pl.when(r + d < n_row)
        def _():
            along(r + d, 1).wait_recv()

            @pl.when(r > 0)
            def _():
                along(r + d, 1).start()

    def lines_drain():
        for copy in map_lines:
            copy.wait_recv()
        for copy in maps + spreads + map_lines:
            copy.wait_send()
        for d in range(n_row):
            @pl.when((r >= d) & (r + 1 < n_row))
            def _():
                along(r - d, 0).wait_send()

            @pl.when((r + d < n_row) & (r > 0))
            def _():
                along(r + d, 1).wait_send()

    def own(k, phase):
        for t in range(CHUNK_TILES):
            for i in range(rows // TILE_ROWS):
                at = pl.ds(i * TILE_ROWS, TILE_ROWS)
                j = k * CHUNK_TILES + t
                codes = codes_ref[at, rows_of(j, HALF)]
                even, odd = lookup(books_ref[map_ref[i, j]], codes)
                left = weights_ref[at, rows_of(2 * j, LANES)].astype(jnp.float32)
                right = weights_ref[at, rows_of(2 * j + 1, LANES)].astype(jnp.float32)
                w_even, w_odd = split_pairs(left, right)
                place = pl.ds(pl.multiple_of(c * rows + i * TILE_ROWS, TILE_ROWS), TILE_ROWS)
                errors[k, place, t * HALF : (t + 1) * HALF] = even - w_even
                errors[k, place, pairs + t * HALF : pairs + (t + 1) * HALF] = odd - w_odd
        cube.pass_on(k, 0, phase)

    def begin(k, phase):
        own(k, phase)
        if isinstance(k, int) and k == 0:
            for copy in spreads + maps + [keep]:
                copy.start()

    nt = min(width, 1024)

    def multiply(slot, columns):
        part_ref[:, columns] += three_products(e_high[...], e_low[...], h_high[slot][:, columns], h_low[slot][:, columns])

    def product(k, slot):
        step = 64

        @pl.when((k >= 0) & (k < chunks))
        def _():
            cube.pair_arrivals(k)

            def convert_error(n, carry):
                place = rows_of(n, step)
                e_high[place, :], e_low[place, :] = halves(errors[k, place, :])
                return carry

            lax.fori_loop(0, errors.shape[1] // step, convert_error, 0)

        @pl.when((k >= 0) & (k + 1 < chunks))
        def _():
            fetched(1 - slot)

            @pl.when(k >= 1)
            def _():
                for copy in out_copies(k - 1, 1 - slot):
                    copy.wait()

            def both(n, carry):
                columns = rows_of(n, nt)
                multiply(slot, columns)
                convert(1 - slot, columns)
                return carry

            lax.fori_loop(0, width // nt, both, 0)
            for copy in out_copies(k + 1, 1 - slot):
                copy.start()

            @pl.when(k + 3 < chunks)
            def _():
                fetch(k + 3, 1 - slot)

        @pl.when(k + 1 == chunks)
        def _():
            def alone(n, carry):
                multiply(slot, rows_of(n, nt))
                return carry

            lax.fori_loop(0, width // nt, alone, 0)

        @pl.when(k == -1)
        def _():
            lines_start()

        for d in range(1, n_row):
            @pl.when(k == (chunks - 1 if d + 1 == n_row else min(2 * d, chunks - 1)))
            def _():
                lines_pass(d)

    def convert_first(n, carry):
        convert(0, rows_of(n, nt))
        return carry

    def prepare():
        fetched(0)
        lax.fori_loop(0, width // nt, convert_first, 0)
        for copy in out_copies(0, 0):
            copy.start()
        if chunks > 2:
            fetch(2, 0)

    cube.turns(chunks, 0, 2, begin, product, prepare)
    for k in range(max(0, chunks - 2), chunks):
        for copy in out_copies(k, k % 2):
            copy.wait()
    lines_drain()
    cube.drain(chunks)


def first_product(n_row, n_col, tile_map, padded, codes, weights, books, hessian):
    rows, length = weights.shape
    count = hessian.shape[0]
    run = hessian.shape[2] * hessian.shape[3]
    width = hessian.shape[1] * run
    size = CHUNK_TILES * TILE_COLS
    chunks = count // size
    total_rows = rows * n_col
    chips = n_col // 2
    dma = pltpu.SemaphoreType.DMA
    whole = jax.ShapeDtypeStruct((chunks, size, width), jnp.bfloat16)
    block = pltpu.VMEM((size, width), jnp.bfloat16)
    return pl.pallas_call(
        functools.partial(first_kernel, n_row, n_col, chunks, run),
        in_specs=[SMEM, VMEM, VMEM, VMEM, VMEM, ANY],
        out_specs=[VMEM, ANY, ANY, ANY, VMEM],
        out_shape=[
            jax.ShapeDtypeStruct((total_rows, width), jnp.float32),
            whole,
            whole,
            jax.ShapeDtypeStruct((n_row, total_rows, max(run // 2, LANES)), jnp.int32),
            jax.ShapeDtypeStruct((n_row, n_col) + padded.shape, jnp.int32),
        ],
        scratch_shapes=[
            pltpu.VMEM((chunks, total_rows, size), jnp.float32),
            pltpu.VMEM((total_rows, size), jnp.bfloat16),
            pltpu.VMEM((total_rows, size), jnp.bfloat16),
            pltpu.VMEM((2, 2, size // 2, width), jnp.float32),
            block,
            block,
            block,
            block,
            dma((chunks, chips)),
            dma((chunks, chips)),
            dma((chunks, chips)),
            dma((chunks, chips)),
            dma((2,)),
            dma((2, 2)),
            dma((n_col,)),
            dma((n_col,)),
            dma,
            dma((2, n_row)),
            dma((2, n_row)),
            dma((n_col,)),
            dma((n_col,)),
            dma((n_row,)),
            dma((n_row,)),
        ],
        compiler_params=pltpu.CompilerParams(collective_id=1, has_side_effects=True, vmem_limit_bytes=VMEM_BYTES),
        cost_estimate=pl.CostEstimate(flops=6 * total_rows * width * count, bytes_accessed=8 * count * width, transcendentals=0),
        name="first_product",
    )(tile_map, padded, codes, weights, books.reshape(-1, 4, LANES), hessian.reshape(count // 2, 2, width // LANES, 1, LANES))


def next_kernel(n_col, chunks, down, map_ref, codes_ref, delta_ref, high_ref, low_ref, part_ref, codes_all, high0, high1, low0, low1, d_high0, d_high1, d_low0, d_low1, hop_send, hop_recv, pair_send, pair_recv, in_sem):
    r, c = lax.axis_index("row"), lax.axis_index("col")
    rows = codes_ref.shape[0]
    total_rows, width = part_ref.shape
    pairs = CHUNK_TILES * HALF
    h_high, h_low = (high0, high1), (low0, low1)
    d_high, d_low = (d_high0, d_high1), (d_low0, d_low1)
    cube = Cube(
        n_col,
        lambda k, at: codes_all.at[k, rows_of(at, rows)],
        lambda k: codes_ref.at[:, rows_of(k, pairs)],
        (hop_send, hop_recv, pair_send, pair_recv),
    )

    def fetch(k, slot):
        return [
            pltpu.make_async_copy(high_ref.at[k], h_high[slot], in_sem.at[slot, 0]),
            pltpu.make_async_copy(low_ref.at[k], h_low[slot], in_sem.at[slot, 1]),
        ]

    for k in range(min(2, chunks)):
        for copy in fetch(k, k):
            copy.start()
    part_ref[...] = jnp.zeros_like(part_ref)
    greet(
        [(r, flip(cube.chip, 1 << d) * 2 + cube.core) for d in range(cube.dims)] + [(r, cube.chip * 2 + 1 - cube.core)]
    )

    def own(k, phase):
        cube.pass_on(k, 0, phase)
        codes_all[k, rows_of(c, rows), :] = codes_ref[:, rows_of(k, pairs)]

    nt = min(width, 1024)
    tiles = total_rows // TILE_ROWS
    share = tiles // (width // nt)

    def look(k, slot, n):
        for q in range(share):
            i = n * share + q
            at = rows_of(i, TILE_ROWS)
            for t in range(CHUNK_TILES):
                codes = codes_all[k, at, t * HALF : (t + 1) * HALF]
                book = map_ref[r, i // down, lax.rem(i, down), k * CHUNK_TILES + t]
                for part, value in enumerate(lookup(delta_ref[book], codes)):
                    high, low = halves(value)
                    left = part * pairs + t * HALF
                    d_high[slot][at, left : left + HALF] = high
                    d_low[slot][at, left : left + HALF] = low

    def multiply(slot, n):
        columns = rows_of(n, nt)
        part_ref[:, columns] += three_products(
            d_high[slot][...], d_low[slot][...], h_high[slot][:, columns], h_low[slot][:, columns]
        )

    def loop(body):
        def one(n, carry):
            body(n)
            return carry

        lax.fori_loop(0, width // nt, one, 0)

    def work(k, slot):
        @pl.when((k >= 0) & (k < chunks))
        def _():
            cube.pair_arrivals(k)

        @pl.when((k >= 1) & (k <= chunks))
        def _():
            for copy in fetch(k - 1, 1 - slot):
                copy.wait()

        @pl.when(k == 0)
        def _():
            loop(lambda n: look(k, slot, n))

        @pl.when((k >= 1) & (k < chunks))
        def _():
            def body(n):
                multiply(1 - slot, n)
                look(k, slot, n)

            loop(body)

        @pl.when(k == chunks)
        def _():
            loop(lambda n: multiply(1 - slot, n))

        @pl.when((k >= 1) & (k + 1 < chunks))
        def _():
            for copy in fetch(k + 1, 1 - slot):
                copy.start()

    cube.turns(chunks, 1, 3, own, work)
    cube.drain(chunks)


def next_product(n_col, down, maps, codes, delta, high, low):
    chunks, size, width = high.shape
    rows = codes.shape[0]
    m = rows * n_col
    chips = n_col // 2
    dma = pltpu.SemaphoreType.DMA
    block = pltpu.VMEM((size, width), jnp.bfloat16)
    factor = pltpu.VMEM((m, size), jnp.bfloat16)
    return pl.pallas_call(
        functools.partial(next_kernel, n_col, chunks, down),
        in_specs=[SMEM, VMEM, VMEM, ANY, ANY],
        out_specs=VMEM,
        out_shape=jax.ShapeDtypeStruct((m, width), jnp.float32),
        scratch_shapes=[pltpu.VMEM((chunks, m, size // 2), jnp.int32)]
        + [block] * 4
        + [factor] * 4
        + [dma((chunks, chips))] * 4
        + [dma((2, 2))],
        compiler_params=pltpu.CompilerParams(collective_id=3, has_side_effects=True, vmem_limit_bytes=VMEM_BYTES),
        cost_estimate=pl.CostEstimate(flops=6 * m * width * size * chunks, bytes_accessed=4 * size * chunks * width, transcendentals=0),
        name="next_product",
    )(maps, codes, delta.reshape(-1, 4, LANES), high, low)


def spread_tile(codes, values):
    upper = codes // LOW
    lower = (codes & (LOW - 1)).astype(jnp.float32).astype(jnp.bfloat16)
    eight = lax.broadcasted_iota(jnp.int32, (8, LANES), 0)
    entry = lax.broadcasted_iota(jnp.int32, (LOW, LANES), 0).astype(jnp.float32).astype(jnp.bfloat16)
    one, zero = jnp.bfloat16(1), jnp.bfloat16(0)
    parts, hots = [], []
    for n in range(TILE_ROWS):
        fits = eight == upper[n : n + 1, :]
        part = jnp.concatenate([jnp.where(fits, x[n : n + 1, :], 0.0) for x in values], axis=0)
        parts.append(part.astype(jnp.bfloat16))
        hots.append(jnp.where(entry == lower[n : n + 1, :], one, zero))
    return lax.dot_general(
        jnp.concatenate(parts, axis=1), jnp.concatenate(hots, axis=1), NT, preferred_element_type=jnp.float32
    )


def scatter_kernel(run, gap, sizes, place_ref, map_ref, codes_ref, grad_ref, books_ref, sums_ref, planes_ref, order_ref):
    g = pl.program_id(0)
    groups, rows_here, span = codes_ref.shape
    down, across = rows_here // TILE_ROWS, groups * span // HALF
    map_down, map_across = sizes
    top = g * down
    begin = place_ref[0]
    halves_apart = run % TILE_COLS != 0
    row = lax.broadcasted_iota(jnp.int32, (8, LOW), 0)

    @pl.when(g == 0)
    def _():
        sums_ref[...] = jnp.zeros_like(sums_ref)
        source = lax.broadcasted_iota(jnp.int32, order_ref.shape, 0)
        target = lax.broadcasted_iota(jnp.int32, order_ref.shape, 1)
        wanted = jnp.where(target < HALF, 2 * target, 2 * (target - HALF) + 1)
        order_ref[...] = jnp.where(source == wanted, 1.0, 0.0).astype(jnp.bfloat16)

    def part(j, carry):
        columns = rows_of(j, TILE_COLS)
        both = jnp.concatenate(halves(grad_ref[:, columns]), axis=0)
        planes_ref[:, columns] = jnp.dot(both, order_ref[...], preferred_element_type=jnp.float32)
        return carry

    lax.fori_loop(0, across, part, 0)

    def book(i, column):
        line = top + i
        tile = ((column // run) * gap + begin + column % run) // TILE_COLS
        return map_ref[tile // map_across, line // map_down, line % map_down, tile % map_across]

    def add(index, sums):
        even, odd = sums[0:8] + sums[8:16], sums[16:24] + sums[24:32]
        first = jnp.where(row < 4, even, jnp.concatenate([odd[4:8], odd[0:4]], axis=0))
        second = jnp.where(row < 4, jnp.concatenate([even[4:8], even[0:4]], axis=0), odd)
        sums_ref[index, :, 0:LOW] += jnp.concatenate([first, second], axis=0)

    def tile(t, carry):
        i, j = t // across, t % across
        rows = rows_of(i, TILE_ROWS)
        codes = codes_ref[j // (span // HALF), rows, rows_of(j % (span // HALF), HALF)]
        low_rows = pl.ds(pl.multiple_of(rows_here + i * TILE_ROWS, TILE_ROWS), TILE_ROWS)
        values = [planes_ref[at, rows_of(2 * j + odd, HALF)] for odd in range(2) for at in (rows, low_rows)]
        if halves_apart:
            left = lax.broadcasted_iota(jnp.int32, codes.shape, 1) < HALF // 2
            add(book(i, j * TILE_COLS), spread_tile(codes, [jnp.where(left, x, 0.0) for x in values]))
            add(book(i, j * TILE_COLS + LANES), spread_tile(codes, [jnp.where(left, 0.0, x) for x in values]))
        else:
            add(book(i, j * TILE_COLS), spread_tile(codes, values))
        return carry

    lax.fori_loop(0, down * across, tile, 0, unroll=1 if halves_apart else 8)

    @pl.when(g == pl.num_programs(0) - 1)
    def _():
        count = sums_ref.shape[0]
        groups = LANES // LOW
        step = 16
        size = step * 4

        def squeeze(n, carry):
            x = sums_ref[rows_of(n, step)].reshape(size, groups, LANES)
            total = x[:, 0, :]
            for b in range(1, groups):
                total = total + pltpu.roll(x[:, b, :], b * LOW, 1)
            books_ref[rows_of(n, size), :] = total
            return carry

        lax.fori_loop(0, count // step, squeeze, 0)


def scatter(run, gap, sizes, begin, maps, codes, grad, shape):
    m, n = grad.shape
    block = min(m, 128)
    return pl.pallas_call(
        functools.partial(scatter_kernel, run, gap, sizes),
        grid=(m // block,),
        in_specs=[
            SMEM,
            SMEM,
            pl.BlockSpec((codes.shape[0], block, codes.shape[2]), lambda i: (0, i, 0)),
            pl.BlockSpec((block, n), lambda i: (i, 0)),
        ],
        out_specs=pl.BlockSpec(shape, lambda i: (0, 0)),
        out_shape=jax.ShapeDtypeStruct(shape, jnp.float32),
        scratch_shapes=[
            pltpu.VMEM((shape[0] // 4, 16, LANES), jnp.float32),
            pltpu.VMEM((2 * block, n), jnp.float32),
            pltpu.VMEM((TILE_COLS, TILE_COLS), jnp.bfloat16),
        ],
        compiler_params=pltpu.CompilerParams(vmem_limit_bytes=VMEM_BYTES),
        cost_estimate=pl.CostEstimate(flops=64 * 32 * m * n, bytes_accessed=6 * m * n, transcendentals=0),
        name="scatter",
    )(begin, maps, codes, grad)


def update_kernel(n_row, n_col, final, grad_ref, books_ref, delta_ref, out_ref, pair_in, pair_sum, chip_in, chip_sum, row_in, *sems):
    r, c = lax.axis_index("row"), lax.axis_index("col")
    chip, core = c // 2, lax.rem(c, 2)
    chips = n_col // 2
    length = grad_ref.shape[0] // PARTS
    half = length // 2
    wide = half // chips
    thin = wide // n_row
    pair = (r, chip * 2 + 1 - core)
    others = [lax.rem(chip + d, chips) for d in range(chips)]
    lines = [lax.rem(r + d, n_row) for d in range(n_row)]
    greet(
        [pair]
        + [(r, others[d] * 2 + core) for d in range(1, chips)]
        + [(lines[d], c) for d in range(1, n_row)]
    )
    started = []

    def send(src, dst, stage, q, d, device):
        copy = pltpu.make_async_remote_copy(
            src_ref=src,
            dst_ref=dst,
            send_sem=sems[2 * stage].at[q, d],
            recv_sem=sems[2 * stage + 1].at[q, d],
            device_id=device,
            device_id_type=MESH,
        )
        copy.start()
        started.append(copy)
        return copy

    def part(q, index, size):
        return pl.ds(pl.multiple_of(q * length + index * size, size), size)

    def received(copies):
        for copy in copies:
            copy.wait_recv()

    def swap(q, before):
        return [send(grad_ref.at[part(q, 1 - core, half)], pair_in.at[q], 0, q, 0, pair)]

    def over_chips(q, before):
        received(before)
        pair_sum[q] = grad_ref[part(q, core, half), :] + pair_in[q]
        return [
            send(pair_sum.at[q, rows_of(others[d], wide)], chip_in.at[q, d], 1, q, d, (r, others[d] * 2 + core))
            for d in range(1, chips)
        ]

    def over_rows(q, before):
        received(before)
        total = pair_sum[q, rows_of(chip, wide), :]
        for d in range(1, chips):
            total = total + chip_in[q, d]
        chip_sum[q] = total
        return [
            send(chip_sum.at[q, rows_of(lines[d], thin)], row_in.at[q, d], 2, q, d, (lines[d], c))
            for d in range(1, n_row)
        ]

    def change(q, before):
        received(before)
        total = chip_sum[q, rows_of(r, thin), :]
        for d in range(1, n_row):
            total = total + row_in[q, d]
        mine = part(q, (core * chips + chip) * n_row + r, thin)
        step = -learn_rate * (2.0 * total)
        if final:
            step = books_ref[mine, :] + (2.0 * delta_ref[mine, :] + step)
        out_ref[mine, :] = step
        return [send(out_ref.at[mine], out_ref.at[mine], 3, q, d, (lines[d], c)) for d in range(1, n_row)]

    def to_chips(q, before):
        received(before)
        piece = part(q, core * chips + chip, wide)
        return [
            send(out_ref.at[piece], out_ref.at[piece], 4, q, d, (r, others[d] * 2 + core)) for d in range(1, chips)
        ]

    def to_pair(q, before):
        received(before)
        piece = part(q, core, half)
        return [send(out_ref.at[piece], out_ref.at[piece], 5, q, 0, pair)]

    before = [[] for _ in range(PARTS)]
    for stage in (swap, over_chips, over_rows, change, to_chips, to_pair):
        for q in range(PARTS):
            before[q] = stage(q, before[q])
    for copies in before:
        received(copies)
    for copy in started:
        copy.wait_send()


def update(n_row, n_col, final, grad, books, delta):
    half = grad.shape[0] // PARTS // 2
    chips = n_col // 2
    wide = half // chips
    thin = wide // n_row
    dma = pltpu.SemaphoreType.DMA
    sizes = [1, chips, n_row, n_row, chips, 1]
    return pl.pallas_call(
        functools.partial(update_kernel, n_row, n_col, final),
        in_specs=[VMEM, VMEM, VMEM],
        out_specs=VMEM,
        out_shape=jax.ShapeDtypeStruct(grad.shape, jnp.float32),
        scratch_shapes=[
            pltpu.VMEM((PARTS, half, LANES), jnp.float32),
            pltpu.VMEM((PARTS, half, LANES), jnp.float32),
            pltpu.VMEM((PARTS, chips, wide, LANES), jnp.float32),
            pltpu.VMEM((PARTS, wide, LANES), jnp.float32),
            pltpu.VMEM((PARTS, n_row, thin, LANES), jnp.float32),
        ]
        + [dma((PARTS, size)) for size in sizes for _ in range(2)],
        compiler_params=pltpu.CompilerParams(collective_id=2 if final else 0, has_side_effects=True),
        name="last_update" if final else "update",
    )(grad, books, delta)


def per_device(n_row, n_col, hessian, weights, codes, tile_map, codebooks):
    count, parts, entries = codebooks.shape
    books = codebooks.reshape(count, parts, entries // LANES, LANES).transpose(0, 2, 1, 3).reshape(-1, LANES)
    run = hessian.shape[2] * hessian.shape[3]
    c = lax.axis_index("col")
    begin = jnp.full((1,), c * run, jnp.int32)
    down, across = tile_map.shape
    padded = jnp.pad(tile_map, ((0, -down % 8), (0, -across % LANES)))

    grad, high, low, spread, maps = first_product(n_row, n_col, tile_map, padded, codes, weights, books, hessian)
    if run // 2 < spread.shape[2]:
        groups, m, span = spread.shape
        spread = lax.dynamic_slice(spread, (0, 0, lax.rem(c * (run // 2), span)), (groups, m, run // 2))
        spread = spread.transpose(1, 0, 2).reshape(1, m, groups * (run // 2))
    split = functools.partial(scatter, run, n_col * run, (down, across), begin, maps, spread)
    delta = update(n_row, n_col, False, split(grad, books.shape), books, books)
    grad = next_product(n_col, down, maps, codes, delta, high, low)
    books = update(n_row, n_col, True, split(grad, books.shape), books, delta)
    return books.reshape(count, entries // LANES, parts, LANES).transpose(0, 2, 1, 3).reshape(codebooks.shape)


def solution(mesh):
    placed = (P("row", None, "col", None), P("col", "row"), P("col", "row"), P("col", "row"), P())
    body = functools.partial(per_device, mesh.shape["row"], mesh.shape["col"])
    return jax.shard_map(body, mesh=mesh, in_specs=placed, out_specs=P(), check_vma=False)
```

```python
import functools

import jax
import jax.numpy as jnp
from jax import lax
from jax.experimental import pallas as pl
from jax.experimental.pallas import tpu as pltpu
from jax.sharding import PartitionSpec as P

TILE_ROWS = 16
TILE_COLS = 256
STEPS = 2
LANES = 128
HALF = TILE_COLS // 2
CHUNK_TILES = 2
LOW = 32
BOOK_LINES = 16

learn_rate = 0.01
MESH = pl.DeviceIdType.MESH
NT = (((1,), (1,)), ((), ()))
VMEM = pl.BlockSpec(memory_space=pltpu.VMEM)
SMEM = pl.BlockSpec(memory_space=pltpu.SMEM)
ANY = pl.BlockSpec(memory_space=pl.ANY)
VMEM_BYTES = 62 * 2**20


def pick(table, index):
    return jnp.take_along_axis(table, index, axis=1, mode="promise_in_bounds")


def lookup(table, code):
    index = code & (LANES - 1)
    upper = code >= LANES
    tables = [jnp.broadcast_to(table[n : n + 1, :], code.shape) for n in range(4)]
    even = jnp.where(upper, pick(tables[2], index), pick(tables[0], index))
    odd = jnp.where(upper, pick(tables[3], index), pick(tables[1], index))
    return even, odd


def split_pairs(left, right):
    lane = lax.broadcasted_iota(jnp.int32, left.shape, 1)
    first = lane < LANES // 2
    index = (2 * lane) & (LANES - 1)
    even = jnp.where(first, pick(left, index), pick(right, index))
    odd = jnp.where(first, pick(left, index + 1), pick(right, index + 1))
    return even, odd


def halves(x):
    high = x.astype(jnp.bfloat16)
    return high, (x - high.astype(jnp.float32)).astype(jnp.bfloat16)


def three_products(a_high, a_low, b_high, b_low):
    dot = functools.partial(jnp.dot, preferred_element_type=jnp.float32)
    return dot(a_high, b_low) + dot(a_low, b_high) + dot(a_high, b_high)


def flip(chip, mask):
    bit = 0
    while mask >> bit:
        if (mask >> bit) & 1:
            size = 1 << bit
            chip = chip + (1 - 2 * lax.rem(chip // size, 2)) * size
        bit += 1
    return chip


def rows_of(index, size):
    return pl.ds(pl.multiple_of(index * size, size), size)


class Cube:
    def __init__(self, n_col, view, first, sems):
        self.r, c = lax.axis_index("row"), lax.axis_index("col")
        self.chip, self.core = c // 2, lax.rem(c, 2)
        self.chips = n_col // 2
        self.dims = self.chips.bit_length() - 1
        self.view, self.first = view, first
        self.hop_send, self.hop_recv, self.pair_send, self.pair_recv = sems

    def order(self, phase):
        return [(phase + i) % self.dims for i in range(self.dims)]

    def last(self, mask, phase):
        return max([i for i, d in enumerate(self.order(phase)) if (mask >> d) & 1], default=-1)

    def block(self, k, mask, core):
        return self.view(k, flip(self.chip, mask) * 2 + core)

    def copy(self, k, mask, target, sends, recvs, device, core):
        here = self.block(k, mask, core)
        return pltpu.make_async_remote_copy(
            src_ref=here if mask or self.first is None else self.first(k),
            dst_ref=here,
            send_sem=sends.at[k, target],
            recv_sem=recvs.at[k, target],
            device_id=device,
            device_id_type=MESH,
        )

    def hop(self, k, mask, target, dim):
        device = (self.r, flip(self.chip, 1 << dim) * 2 + self.core)
        return self.copy(k, mask, target, self.hop_send, self.hop_recv, device, self.core)

    def across(self, k, mask):
        device = (self.r, self.chip * 2 + 1 - self.core)
        return self.copy(k, mask, mask, self.pair_send, self.pair_recv, device, self.core)

    def pass_on(self, k, mask, phase):
        for i in range(self.last(mask, phase) + 1, self.dims):
            dim = self.order(phase)[i]
            self.hop(k, mask, mask | (1 << dim), dim).start()
        self.across(k, mask).start()

    def arrivals(self, k, level, phase):
        for mask in range(1, self.chips):
            if mask.bit_count() == level:
                self.hop(k, mask, mask, self.order(phase)[self.last(mask, phase)]).wait_recv()
                self.pass_on(k, mask, phase)

    def pair_arrivals(self, k):
        device = (self.r, self.chip * 2 + 1 - self.core)
        for mask in range(self.chips):
            self.copy(k, mask, mask, self.pair_send, self.pair_recv, device, 1 - self.core).wait_recv()

    def drain(self, chunks):
        def one(k, carry):
            for mask in range(self.chips):
                self.across(k, mask).wait_send()
                if mask:
                    self.hop(k, mask, mask, 0).wait_send()
            return carry

        lax.fori_loop(0, chunks, one, 0)

    def turns(self, chunks, extra, ahead, begin, work, prepare=lambda: None):
        unroll = self.dims * (1 + self.dims % 2)
        count = chunks + self.dims + extra
        for k in range(min(ahead, chunks)):
            begin(k, k)
        prepare()

        def turn(step, carry):
            for u in range(unroll):
                t = step * unroll + u

                for level in range(self.dims, 0, -1):
                    k = t - level + 1

                    @pl.when((k >= 0) & (k < chunks))
                    def _():
                        self.arrivals(k, level, (u - level + 1) % self.dims)

                @pl.when(t + ahead < chunks)
                def _():
                    begin(t + ahead, u + ahead)

                work(t - self.dims, (u - self.dims) % 2)
            return carry

        lax.fori_loop(0, -(-count // unroll), turn, 0)


def greet(devices):
    barrier = pltpu.get_barrier_semaphore()
    for device in devices:
        pl.semaphore_signal(barrier, inc=1, device_id=device, device_id_type=MESH)
    pl.semaphore_wait(barrier, len(devices))


def first_kernel(n_row, n_col, chunks, run, map_ref, padded_ref, codes_ref, weights_ref, books_ref, hessian_ref, part_ref, high_out, low_out, spread_out, maps_out, errors, e_high, e_low, h_in, high0, high1, low0, low1, hop_send, hop_recv, pair_send, pair_recv, in_sem, out_sem, code_send, code_recv, own_sem, line_send, line_recv, map_send, map_recv, map_send2, map_recv2):
    r, c = lax.axis_index("row"), lax.axis_index("col")
    rows = codes_ref.shape[0]
    width = h_in.shape[3]
    pairs = CHUNK_TILES * HALF
    h_high, h_low = (high0, high1), (low0, low1)
    cols = [lax.rem(c + d, n_col) for d in range(n_col)]
    lines = [lax.rem(r + d, n_row) for d in range(n_row)]
    cube = Cube(n_col, lambda k, at: errors.at[k, rows_of(at, rows)], None, (hop_send, hop_recv, pair_send, pair_recv))

    def fetch(k, slot):
        def one(n, carry):
            for parity in range(2):
                pltpu.make_async_copy(
                    hessian_ref.at[rows_of(k, pairs), parity, n, 0],
                    h_in.at[slot, parity, :, rows_of(n, LANES)],
                    in_sem.at[slot],
                ).start()
            return carry

        lax.fori_loop(0, width // LANES, one, 0)

    def fetched(slot):
        pltpu.make_async_copy(h_in.at[slot], h_in.at[slot], in_sem.at[slot]).wait()

    def out_copies(k, slot):
        return [
            pltpu.make_async_copy(h_high[slot], high_out.at[k], out_sem.at[slot, 0]),
            pltpu.make_async_copy(h_low[slot], low_out.at[k], out_sem.at[slot, 1]),
        ]

    def convert(slot, columns):
        for parity in range(2):
            high, low = halves(h_in[slot, parity, :, columns])
            h_high[slot][parity * pairs : (parity + 1) * pairs, columns] = high
            h_low[slot][parity * pairs : (parity + 1) * pairs, columns] = low

    fetch(0, 0)
    if chunks > 1:
        fetch(1, 1)
    part_ref[...] = jnp.zeros_like(part_ref)
    maps_out[r, c] = padded_ref[...]
    greet([(r, cols[d]) for d in range(1, n_col)] + [(lines[d], c) for d in range(1, n_row)])

    span = max(run // 2, LANES)

    def piece(at):
        return codes_ref.at[:, rows_of(at * (run // 2) // span, span)]

    def send(src, dst, sends, recvs, d, device):
        return pltpu.make_async_remote_copy(
            src_ref=src, dst_ref=dst, send_sem=sends.at[d], recv_sem=recvs.at[d], device_id=device, device_id_type=MESH
        )

    here = spread_out.at[r, rows_of(c, rows)]
    spreads = [send(piece(cols[d]), here, code_send, code_recv, d, (r, cols[d])) for d in range(1, n_col)]
    maps = [send(padded_ref, maps_out.at[r, c], map_send, map_recv, d, (r, cols[d])) for d in range(1, n_col)]
    map_lines = [send(maps_out.at[r], maps_out.at[r], map_send2, map_recv2, d, (lines[d], c)) for d in range(1, n_row)]
    keep = pltpu.make_async_copy(piece(c), here, own_sem)

    def along(at, way):
        return pltpu.make_async_remote_copy(
            src_ref=spread_out.at[at],
            dst_ref=spread_out.at[at],
            send_sem=line_send.at[way, at],
            recv_sem=line_recv.at[way, at],
            device_id=(r + 1 - 2 * way, c),
            device_id_type=MESH,
        )

    def lines_start():
        for copy in maps + spreads:
            copy.wait_recv()
        keep.wait()
        for copy in map_lines:
            copy.start()

        @pl.when(r + 1 < n_row)
        def _():
            along(r, 0).start()

        @pl.when(r > 0)
        def _():
            along(r, 1).start()

    def lines_pass(d):
        @pl.when(r >= d)
        def _():
            along(r - d, 0).wait_recv()

            @pl.when(r + 1 < n_row)
            def _():
                along(r - d, 0).start()

        @pl.when(r + d < n_row)
        def _():
            along(r + d, 1).wait_recv()

            @pl.when(r > 0)
            def _():
                along(r + d, 1).start()

    def lines_drain():
        for copy in map_lines:
            copy.wait_recv()
        for copy in maps + spreads + map_lines:
            copy.wait_send()
        for d in range(n_row):
            @pl.when((r >= d) & (r + 1 < n_row))
            def _():
                along(r - d, 0).wait_send()

            @pl.when((r + d < n_row) & (r > 0))
            def _():
                along(r + d, 1).wait_send()

    def own(k, phase):
        for t in range(CHUNK_TILES):
            for i in range(rows // TILE_ROWS):
                at = pl.ds(i * TILE_ROWS, TILE_ROWS)
                j = k * CHUNK_TILES + t
                codes = codes_ref[at, rows_of(j, HALF)]
                even, odd = lookup(books_ref[map_ref[i, j]], codes)
                left = weights_ref[at, rows_of(2 * j, LANES)].astype(jnp.float32)
                right = weights_ref[at, rows_of(2 * j + 1, LANES)].astype(jnp.float32)
                w_even, w_odd = split_pairs(left, right)
                place = pl.ds(pl.multiple_of(c * rows + i * TILE_ROWS, TILE_ROWS), TILE_ROWS)
                errors[k, place, t * HALF : (t + 1) * HALF] = even - w_even
                errors[k, place, pairs + t * HALF : pairs + (t + 1) * HALF] = odd - w_odd
        cube.pass_on(k, 0, phase)

    def begin(k, phase):
        own(k, phase)
        if isinstance(k, int) and k == 0:
            for copy in spreads + maps + [keep]:
                copy.start()

    nt = min(width, 1024)

    def multiply(slot, columns):
        part_ref[:, columns] += three_products(e_high[...], e_low[...], h_high[slot][:, columns], h_low[slot][:, columns])

    def product(k, slot):
        step = 64

        @pl.when((k >= 0) & (k < chunks))
        def _():
            cube.pair_arrivals(k)

            def convert_error(n, carry):
                place = rows_of(n, step)
                e_high[place, :], e_low[place, :] = halves(errors[k, place, :])
                return carry

            lax.fori_loop(0, errors.shape[1] // step, convert_error, 0)

        @pl.when((k >= 0) & (k + 1 < chunks))
        def _():
            fetched(1 - slot)

            @pl.when(k >= 1)
            def _():
                for copy in out_copies(k - 1, 1 - slot):
                    copy.wait()

            def both(n, carry):
                columns = rows_of(n, nt)
                multiply(slot, columns)
                convert(1 - slot, columns)
                return carry

            lax.fori_loop(0, width // nt, both, 0)
            for copy in out_copies(k + 1, 1 - slot):
                copy.start()

            @pl.when(k + 3 < chunks)
            def _():
                fetch(k + 3, 1 - slot)

        @pl.when(k + 1 == chunks)
        def _():
            def alone(n, carry):
                multiply(slot, rows_of(n, nt))
                return carry

            lax.fori_loop(0, width // nt, alone, 0)

        @pl.when(k == -1)
        def _():
            lines_start()

        for d in range(1, n_row):
            @pl.when(k == (chunks - 1 if d + 1 == n_row else min(2 * d, chunks - 1)))
            def _():
                lines_pass(d)

    def convert_first(n, carry):
        convert(0, rows_of(n, nt))
        return carry

    def prepare():
        fetched(0)
        lax.fori_loop(0, width // nt, convert_first, 0)
        for copy in out_copies(0, 0):
            copy.start()
        if chunks > 2:
            fetch(2, 0)

    cube.turns(chunks, 0, 2, begin, product, prepare)
    for k in range(max(0, chunks - 2), chunks):
        for copy in out_copies(k, k % 2):
            copy.wait()
    lines_drain()
    cube.drain(chunks)


def first_product(n_row, n_col, tile_map, padded, codes, weights, books, hessian):
    rows, length = weights.shape
    count = hessian.shape[0]
    run = hessian.shape[2] * hessian.shape[3]
    width = hessian.shape[1] * run
    size = CHUNK_TILES * TILE_COLS
    chunks = count // size
    total_rows = rows * n_col
    chips = n_col // 2
    dma = pltpu.SemaphoreType.DMA
    whole = jax.ShapeDtypeStruct((chunks, size, width), jnp.bfloat16)
    block = pltpu.VMEM((size, width), jnp.bfloat16)
    return pl.pallas_call(
        functools.partial(first_kernel, n_row, n_col, chunks, run),
        in_specs=[SMEM, VMEM, VMEM, VMEM, VMEM, ANY],
        out_specs=[VMEM, ANY, ANY, ANY, VMEM],
        out_shape=[
            jax.ShapeDtypeStruct((total_rows, width), jnp.float32),
            whole,
            whole,
            jax.ShapeDtypeStruct((n_row, total_rows, max(run // 2, LANES)), jnp.int32),
            jax.ShapeDtypeStruct((n_row, n_col) + padded.shape, jnp.int32),
        ],
        scratch_shapes=[
            pltpu.VMEM((chunks, total_rows, size), jnp.float32),
            pltpu.VMEM((total_rows, size), jnp.bfloat16),
            pltpu.VMEM((total_rows, size), jnp.bfloat16),
            pltpu.VMEM((2, 2, size // 2, width), jnp.float32),
            block,
            block,
            block,
            block,
            dma((chunks, chips)),
            dma((chunks, chips)),
            dma((chunks, chips)),
            dma((chunks, chips)),
            dma((2,)),
            dma((2, 2)),
            dma((n_col,)),
            dma((n_col,)),
            dma,
            dma((2, n_row)),
            dma((2, n_row)),
            dma((n_col,)),
            dma((n_col,)),
            dma((n_row,)),
            dma((n_row,)),
        ],
        compiler_params=pltpu.CompilerParams(collective_id=1, has_side_effects=True, vmem_limit_bytes=VMEM_BYTES),
        cost_estimate=pl.CostEstimate(flops=6 * total_rows * width * count, bytes_accessed=8 * count * width, transcendentals=0),
        name="first_product",
    )(tile_map, padded, codes, weights, books.reshape(-1, 4, LANES), hessian.reshape(count // 2, 2, width // LANES, 1, LANES))


def next_kernel(n_col, chunks, down, map_ref, codes_ref, delta_ref, high_ref, low_ref, part_ref, codes_all, high0, high1, low0, low1, d_high0, d_high1, d_low0, d_low1, hop_send, hop_recv, pair_send, pair_recv, in_sem):
    r, c = lax.axis_index("row"), lax.axis_index("col")
    rows = codes_ref.shape[0]
    total_rows, width = part_ref.shape
    pairs = CHUNK_TILES * HALF
    h_high, h_low = (high0, high1), (low0, low1)
    d_high, d_low = (d_high0, d_high1), (d_low0, d_low1)
    cube = Cube(
        n_col,
        lambda k, at: codes_all.at[k, rows_of(at, rows)],
        lambda k: codes_ref.at[:, rows_of(k, pairs)],
        (hop_send, hop_recv, pair_send, pair_recv),
    )

    def fetch(k, slot):
        return [
            pltpu.make_async_copy(high_ref.at[k], h_high[slot], in_sem.at[slot, 0]),
            pltpu.make_async_copy(low_ref.at[k], h_low[slot], in_sem.at[slot, 1]),
        ]

    for k in range(min(2, chunks)):
        for copy in fetch(k, k):
            copy.start()
    part_ref[...] = jnp.zeros_like(part_ref)
    greet(
        [(r, flip(cube.chip, 1 << d) * 2 + cube.core) for d in range(cube.dims)] + [(r, cube.chip * 2 + 1 - cube.core)]
    )

    def own(k, phase):
        cube.pass_on(k, 0, phase)
        codes_all[k, rows_of(c, rows), :] = codes_ref[:, rows_of(k, pairs)]

    nt = min(width, 1024)
    tiles = total_rows // TILE_ROWS
    share = tiles // (width // nt)

    def look(k, slot, n):
        for q in range(share):
            i = n * share + q
            at = rows_of(i, TILE_ROWS)
            for t in range(CHUNK_TILES):
                codes = codes_all[k, at, t * HALF : (t + 1) * HALF]
                book = map_ref[r, i // down, lax.rem(i, down), k * CHUNK_TILES + t]
                for part, value in enumerate(lookup(delta_ref[book], codes)):
                    high, low = halves(value)
                    left = part * pairs + t * HALF
                    d_high[slot][at, left : left + HALF] = high
                    d_low[slot][at, left : left + HALF] = low

    def multiply(slot, n):
        columns = rows_of(n, nt)
        part_ref[:, columns] += three_products(
            d_high[slot][...], d_low[slot][...], h_high[slot][:, columns], h_low[slot][:, columns]
        )

    def loop(body):
        def one(n, carry):
            body(n)
            return carry

        lax.fori_loop(0, width // nt, one, 0)

    def work(k, slot):
        @pl.when((k >= 0) & (k < chunks))
        def _():
            cube.pair_arrivals(k)

        @pl.when((k >= 1) & (k <= chunks))
        def _():
            for copy in fetch(k - 1, 1 - slot):
                copy.wait()

        @pl.when(k == 0)
        def _():
            loop(lambda n: look(k, slot, n))

        @pl.when((k >= 1) & (k < chunks))
        def _():
            def body(n):
                multiply(1 - slot, n)
                look(k, slot, n)

            loop(body)

        @pl.when(k == chunks)
        def _():
            loop(lambda n: multiply(1 - slot, n))

        @pl.when((k >= 1) & (k + 1 < chunks))
        def _():
            for copy in fetch(k + 1, 1 - slot):
                copy.start()

    cube.turns(chunks, 1, 2, own, work)
    cube.drain(chunks)


def next_product(n_col, down, maps, codes, delta, high, low):
    chunks, size, width = high.shape
    rows = codes.shape[0]
    m = rows * n_col
    chips = n_col // 2
    dma = pltpu.SemaphoreType.DMA
    block = pltpu.VMEM((size, width), jnp.bfloat16)
    factor = pltpu.VMEM((m, size), jnp.bfloat16)
    return pl.pallas_call(
        functools.partial(next_kernel, n_col, chunks, down),
        in_specs=[SMEM, VMEM, VMEM, ANY, ANY],
        out_specs=VMEM,
        out_shape=jax.ShapeDtypeStruct((m, width), jnp.float32),
        scratch_shapes=[pltpu.VMEM((chunks, m, size // 2), jnp.int32)]
        + [block] * 4
        + [factor] * 4
        + [dma((chunks, chips))] * 4
        + [dma((2, 2))],
        compiler_params=pltpu.CompilerParams(collective_id=3, has_side_effects=True, vmem_limit_bytes=VMEM_BYTES),
        cost_estimate=pl.CostEstimate(flops=6 * m * width * size * chunks, bytes_accessed=4 * size * chunks * width, transcendentals=0),
        name="next_product",
    )(maps, codes, delta.reshape(-1, 4, LANES), high, low)


def spread_tile(codes, values):
    upper = codes // LOW
    lower = (codes & (LOW - 1)).astype(jnp.float32).astype(jnp.bfloat16)
    eight = lax.broadcasted_iota(jnp.int32, (8, LANES), 0)
    entry = lax.broadcasted_iota(jnp.int32, (LOW, LANES), 0).astype(jnp.float32).astype(jnp.bfloat16)
    one, zero = jnp.bfloat16(1), jnp.bfloat16(0)
    parts, hots = [], []
    for n in range(TILE_ROWS):
        fits = eight == upper[n : n + 1, :]
        part = jnp.concatenate([jnp.where(fits, x[n : n + 1, :], 0.0) for x in values], axis=0)
        parts.append(part.astype(jnp.bfloat16))
        hots.append(jnp.where(entry == lower[n : n + 1, :], one, zero))
    return lax.dot_general(
        jnp.concatenate(parts, axis=1), jnp.concatenate(hots, axis=1), NT, preferred_element_type=jnp.float32
    )


def scatter_kernel(run, gap, sizes, place_ref, map_ref, codes_ref, grad_ref, books_ref, sums_ref, planes_ref, order_ref):
    g = pl.program_id(0)
    groups, rows_here, span = codes_ref.shape
    down, across = rows_here // TILE_ROWS, groups * span // HALF
    map_down, map_across = sizes
    top = g * down
    begin = place_ref[0]
    halves_apart = run % TILE_COLS != 0
    row = lax.broadcasted_iota(jnp.int32, (8, LOW), 0)

    @pl.when(g == 0)
    def _():
        sums_ref[...] = jnp.zeros_like(sums_ref)
        source = lax.broadcasted_iota(jnp.int32, order_ref.shape, 0)
        target = lax.broadcasted_iota(jnp.int32, order_ref.shape, 1)
        wanted = jnp.where(target < HALF, 2 * target, 2 * (target - HALF) + 1)
        order_ref[...] = jnp.where(source == wanted, 1.0, 0.0).astype(jnp.bfloat16)

    def part(j, carry):
        columns = rows_of(j, TILE_COLS)
        both = jnp.concatenate(halves(grad_ref[:, columns]), axis=0)
        planes_ref[:, columns] = jnp.dot(both, order_ref[...], preferred_element_type=jnp.float32)
        return carry

    lax.fori_loop(0, across, part, 0)

    def book(i, column):
        line = top + i
        tile = ((column // run) * gap + begin + column % run) // TILE_COLS
        return map_ref[tile // map_across, line // map_down, line % map_down, tile % map_across]

    def add(index, sums):
        even, odd = sums[0:8] + sums[8:16], sums[16:24] + sums[24:32]
        first = jnp.where(row < 4, even, jnp.concatenate([odd[4:8], odd[0:4]], axis=0))
        second = jnp.where(row < 4, jnp.concatenate([even[4:8], even[0:4]], axis=0), odd)
        sums_ref[rows_of(index, BOOK_LINES), 0:LOW] += jnp.concatenate([first, second], axis=0)

    def tile(t, carry):
        i, j = t // across, t % across
        rows = rows_of(i, TILE_ROWS)
        codes = codes_ref[j // (span // HALF), rows, rows_of(j % (span // HALF), HALF)]
        low_rows = pl.ds(pl.multiple_of(rows_here + i * TILE_ROWS, TILE_ROWS), TILE_ROWS)
        values = [planes_ref[at, rows_of(2 * j + odd, HALF)] for odd in range(2) for at in (rows, low_rows)]
        if halves_apart:
            left = lax.broadcasted_iota(jnp.int32, codes.shape, 1) < HALF // 2
            add(book(i, j * TILE_COLS), spread_tile(codes, [jnp.where(left, x, 0.0) for x in values]))
            add(book(i, j * TILE_COLS + LANES), spread_tile(codes, [jnp.where(left, 0.0, x) for x in values]))
        else:
            add(book(i, j * TILE_COLS), spread_tile(codes, values))
        return carry

    lax.fori_loop(0, down * across, tile, 0, unroll=1 if halves_apart else 8)

    @pl.when(g == pl.num_programs(0) - 1)
    def _():
        groups = LANES // LOW
        size = 64

        def squeeze(n, carry):
            at = pl.multiple_of(n * size * groups, size * groups)
            total = sums_ref[pl.ds(at, size, stride=groups), :]
            for b in range(1, groups):
                total = total + pltpu.roll(sums_ref[pl.ds(at + b, size, stride=groups), :], b * LOW, 1)
            books_ref[rows_of(n, size), :] = total
            return carry

        lax.fori_loop(0, books_ref.shape[0] // size, squeeze, 0)


def scatter(run, gap, sizes, begin, maps, codes, grad, shape):
    m, n = grad.shape
    block = min(m, 128)
    return pl.pallas_call(
        functools.partial(scatter_kernel, run, gap, sizes),
        grid=(m // block,),
        in_specs=[
            SMEM,
            SMEM,
            pl.BlockSpec((codes.shape[0], block, codes.shape[2]), lambda i: (0, i, 0)),
            pl.BlockSpec((block, n), lambda i: (i, 0)),
        ],
        out_specs=pl.BlockSpec(shape, lambda i: (0, 0)),
        out_shape=jax.ShapeDtypeStruct(shape, jnp.float32),
        scratch_shapes=[
            pltpu.VMEM((shape[0] // 4 * BOOK_LINES, LANES), jnp.float32),
            pltpu.VMEM((2 * block, n), jnp.float32),
            pltpu.VMEM((TILE_COLS, TILE_COLS), jnp.bfloat16),
        ],
        compiler_params=pltpu.CompilerParams(vmem_limit_bytes=VMEM_BYTES),
        cost_estimate=pl.CostEstimate(flops=64 * 32 * m * n, bytes_accessed=6 * m * n, transcendentals=0),
        name="scatter",
    )(begin, maps, codes, grad)


def update_kernel(n_row, n_col, parts, grad_ref, out_ref, pair_in, pair_sum, chip_in, chip_sum, row_in, *sems):
    r, c = lax.axis_index("row"), lax.axis_index("col")
    chip, core = c // 2, lax.rem(c, 2)
    chips = n_col // 2
    length = grad_ref.shape[0] // parts
    half = length // 2
    wide = half // chips
    thin = wide // n_row
    pair = (r, chip * 2 + 1 - core)
    others = [lax.rem(chip + d, chips) for d in range(chips)]
    lines = [lax.rem(r + d, n_row) for d in range(n_row)]
    greet(
        [pair]
        + [(r, others[d] * 2 + core) for d in range(1, chips)]
        + [(lines[d], c) for d in range(1, n_row)]
    )
    started = []

    def send(src, dst, stage, q, d, device):
        copy = pltpu.make_async_remote_copy(
            src_ref=src,
            dst_ref=dst,
            send_sem=sems[2 * stage].at[q, d],
            recv_sem=sems[2 * stage + 1].at[q, d],
            device_id=device,
            device_id_type=MESH,
        )
        copy.start()
        started.append(copy)
        return copy

    def part(q, index, size):
        return pl.ds(pl.multiple_of(q * length + index * size, size), size)

    def received(copies):
        for copy in copies:
            copy.wait_recv()

    def swap(q, before):
        return [send(grad_ref.at[part(q, 1 - core, half)], pair_in.at[q], 0, q, 0, pair)]

    def over_chips(q, before):
        received(before)
        pair_sum[q] = grad_ref[part(q, core, half), :] + pair_in[q]
        return [
            send(pair_sum.at[q, rows_of(others[d], wide)], chip_in.at[q, d], 1, q, d, (r, others[d] * 2 + core))
            for d in range(1, chips)
        ]

    def over_rows(q, before):
        received(before)
        total = pair_sum[q, rows_of(chip, wide), :]
        for d in range(1, chips):
            total = total + chip_in[q, d]
        chip_sum[q] = total
        return [
            send(chip_sum.at[q, rows_of(lines[d], thin)], row_in.at[q, d], 2, q, d, (lines[d], c))
            for d in range(1, n_row)
        ]

    def change(q, before):
        received(before)
        total = chip_sum[q, rows_of(r, thin), :]
        for d in range(1, n_row):
            total = total + row_in[q, d]
        mine = part(q, (core * chips + chip) * n_row + r, thin)
        out_ref[mine, :] = -learn_rate * (2.0 * total)
        return [send(out_ref.at[mine], out_ref.at[mine], 3, q, d, (lines[d], c)) for d in range(1, n_row)]

    def to_chips(q, before):
        received(before)
        piece = part(q, core * chips + chip, wide)
        return [
            send(out_ref.at[piece], out_ref.at[piece], 4, q, d, (r, others[d] * 2 + core)) for d in range(1, chips)
        ]

    def to_pair(q, before):
        received(before)
        piece = part(q, core, half)
        return [send(out_ref.at[piece], out_ref.at[piece], 5, q, 0, pair)]

    before = [[] for _ in range(parts)]
    for stage in (swap, over_chips, over_rows, change, to_chips, to_pair):
        for q in range(parts):
            before[q] = stage(q, before[q])
    for copies in before:
        received(copies)
    for copy in started:
        copy.wait_send()


def update(n_row, n_col, grad):
    chips = n_col // 2
    parts = 4 if grad.shape[0] % (4 * 2 * chips * n_row * 8) == 0 else 2
    half = grad.shape[0] // parts // 2
    wide = half // chips
    thin = wide // n_row
    dma = pltpu.SemaphoreType.DMA
    sizes = [1, chips, n_row, n_row, chips, 1]
    return pl.pallas_call(
        functools.partial(update_kernel, n_row, n_col, parts),
        in_specs=[VMEM],
        out_specs=VMEM,
        out_shape=jax.ShapeDtypeStruct(grad.shape, jnp.float32),
        scratch_shapes=[
            pltpu.VMEM((parts, half, LANES), jnp.float32),
            pltpu.VMEM((parts, half, LANES), jnp.float32),
            pltpu.VMEM((parts, chips, wide, LANES), jnp.float32),
            pltpu.VMEM((parts, wide, LANES), jnp.float32),
            pltpu.VMEM((parts, n_row, thin, LANES), jnp.float32),
        ]
        + [dma((parts, size)) for size in sizes for _ in range(2)],
        compiler_params=pltpu.CompilerParams(collective_id=0, has_side_effects=True),
        name="update",
    )(grad)


def per_device(n_row, n_col, hessian, weights, codes, tile_map, codebooks):
    count, parts, entries = codebooks.shape
    books = codebooks.reshape(count, parts, entries // LANES, LANES).transpose(0, 2, 1, 3).reshape(-1, LANES)
    run = hessian.shape[2] * hessian.shape[3]
    c = lax.axis_index("col")
    begin = jnp.full((1,), c * run, jnp.int32)
    down, across = tile_map.shape
    padded = jnp.pad(tile_map, ((0, -down % 8), (0, -across % LANES)))

    grad, high, low, spread, maps = first_product(n_row, n_col, tile_map, padded, codes, weights, books, hessian)
    if run // 2 < spread.shape[2]:
        groups, m, span = spread.shape
        spread = lax.dynamic_slice(spread, (0, 0, lax.rem(c * (run // 2), span)), (groups, m, run // 2))
        spread = spread.transpose(1, 0, 2).reshape(1, m, groups * (run // 2))
    split = functools.partial(scatter, run, n_col * run, (down, across), begin, maps, spread)
    delta = update(n_row, n_col, split(grad, books.shape))
    grad = next_product(n_col, down, maps, codes, delta, high, low)
    books = books + (2.0 * delta + update(n_row, n_col, split(grad, books.shape)))
    return books.reshape(count, entries // LANES, parts, LANES).transpose(0, 2, 1, 3).reshape(codebooks.shape)


def solution(mesh):
    placed = (P("row", None, "col", None), P("col", "row"), P("col", "row"), P("col", "row"), P())
    body = functools.partial(per_device, mesh.shape["row"], mesh.shape["col"])
    return jax.shard_map(body, mesh=mesh, in_specs=placed, out_specs=P(), check_vma=False)
```

```python
import functools

import jax
import jax.numpy as jnp
from jax import lax
from jax.experimental import pallas as pl
from jax.experimental.pallas import tpu as pltpu
from jax.sharding import PartitionSpec as P

TILE_ROWS = 16
TILE_COLS = 256
STEPS = 2
LANES = 128
HALF = TILE_COLS // 2
CHUNK_TILES = 2
LOW = 32
BOOK_LINES = 16

learn_rate = 0.01
MESH = pl.DeviceIdType.MESH
NT = (((1,), (1,)), ((), ()))
VMEM = pl.BlockSpec(memory_space=pltpu.VMEM)
SMEM = pl.BlockSpec(memory_space=pltpu.SMEM)
ANY = pl.BlockSpec(memory_space=pl.ANY)
VMEM_BYTES = 62 * 2**20


def pick(table, index):
    return jnp.take_along_axis(table, index, axis=1, mode="promise_in_bounds")


def lookup(table, code):
    index = code & (LANES - 1)
    upper = code >= LANES
    tables = [jnp.broadcast_to(table[n : n + 1, :], code.shape) for n in range(4)]
    even = jnp.where(upper, pick(tables[2], index), pick(tables[0], index))
    odd = jnp.where(upper, pick(tables[3], index), pick(tables[1], index))
    return even, odd


def split_pairs(left, right):
    lane = lax.broadcasted_iota(jnp.int32, left.shape, 1)
    first = lane < LANES // 2
    index = (2 * lane) & (LANES - 1)
    even = jnp.where(first, pick(left, index), pick(right, index))
    odd = jnp.where(first, pick(left, index + 1), pick(right, index + 1))
    return even, odd


def halves(x):
    high = x.astype(jnp.bfloat16)
    return high, (x - high.astype(jnp.float32)).astype(jnp.bfloat16)


def three_products(a_high, a_low, b_high, b_low):
    dot = functools.partial(jnp.dot, preferred_element_type=jnp.float32)
    return dot(a_high, b_low) + dot(a_low, b_high) + dot(a_high, b_high)


def flip(chip, mask):
    bit = 0
    while mask >> bit:
        if (mask >> bit) & 1:
            size = 1 << bit
            chip = chip + (1 - 2 * lax.rem(chip // size, 2)) * size
        bit += 1
    return chip


def rows_of(index, size):
    return pl.ds(pl.multiple_of(index * size, size), size)


class Cube:
    def __init__(self, n_col, view, first, sems):
        self.r, c = lax.axis_index("row"), lax.axis_index("col")
        self.chip, self.core = c // 2, lax.rem(c, 2)
        self.chips = n_col // 2
        self.dims = self.chips.bit_length() - 1
        self.view, self.first = view, first
        self.hop_send, self.hop_recv, self.pair_send, self.pair_recv = sems

    def order(self, phase):
        return [(phase + i) % self.dims for i in range(self.dims)]

    def last(self, mask, phase):
        return max([i for i, d in enumerate(self.order(phase)) if (mask >> d) & 1], default=-1)

    def block(self, k, mask, core):
        return self.view(k, flip(self.chip, mask) * 2 + core)

    def copy(self, k, mask, target, sends, recvs, device, core):
        here = self.block(k, mask, core)
        return pltpu.make_async_remote_copy(
            src_ref=here if mask or self.first is None else self.first(k),
            dst_ref=here,
            send_sem=sends.at[k, target],
            recv_sem=recvs.at[k, target],
            device_id=device,
            device_id_type=MESH,
        )

    def hop(self, k, mask, target, dim):
        device = (self.r, flip(self.chip, 1 << dim) * 2 + self.core)
        return self.copy(k, mask, target, self.hop_send, self.hop_recv, device, self.core)

    def across(self, k, mask):
        device = (self.r, self.chip * 2 + 1 - self.core)
        return self.copy(k, mask, mask, self.pair_send, self.pair_recv, device, self.core)

    def pass_on(self, k, mask, phase):
        for i in range(self.last(mask, phase) + 1, self.dims):
            dim = self.order(phase)[i]
            self.hop(k, mask, mask | (1 << dim), dim).start()
        self.across(k, mask).start()

    def arrivals(self, k, level, phase):
        for mask in range(1, self.chips):
            if mask.bit_count() == level:
                self.hop(k, mask, mask, self.order(phase)[self.last(mask, phase)]).wait_recv()
                self.pass_on(k, mask, phase)

    def pair_arrivals(self, k):
        device = (self.r, self.chip * 2 + 1 - self.core)
        for mask in range(self.chips):
            self.copy(k, mask, mask, self.pair_send, self.pair_recv, device, 1 - self.core).wait_recv()

    def drain(self, chunks):
        def one(k, carry):
            for mask in range(self.chips):
                self.across(k, mask).wait_send()
                if mask:
                    self.hop(k, mask, mask, 0).wait_send()
            return carry

        lax.fori_loop(0, chunks, one, 0)

    def turns(self, chunks, extra, ahead, begin, work, prepare=lambda: None):
        unroll = self.dims * (1 + self.dims % 2)
        count = chunks + self.dims + extra
        for k in range(min(ahead, chunks)):
            begin(k, k)
        prepare()

        def turn(step, carry):
            for u in range(unroll):
                t = step * unroll + u

                for level in range(self.dims, 0, -1):
                    k = t - level + 1

                    @pl.when((k >= 0) & (k < chunks))
                    def _():
                        self.arrivals(k, level, (u - level + 1) % self.dims)

                @pl.when(t + ahead < chunks)
                def _():
                    begin(t + ahead, u + ahead)

                work(t - self.dims, (u - self.dims) % 2)
            return carry

        lax.fori_loop(0, -(-count // unroll), turn, 0)


def greet(devices):
    barrier = pltpu.get_barrier_semaphore()
    for device in devices:
        pl.semaphore_signal(barrier, inc=1, device_id=device, device_id_type=MESH)
    pl.semaphore_wait(barrier, len(devices))


def first_kernel(n_row, n_col, chunks, run, map_ref, padded_ref, codes_ref, weights_ref, books_ref, hessian_ref, part_ref, high_out, low_out, spread_out, maps_out, errors, e_high, e_low, h_in, high0, high1, low0, low1, hop_send, hop_recv, pair_send, pair_recv, in_sem, out_sem, code_send, code_recv, own_sem, line_send, line_recv, map_send, map_recv, map_send2, map_recv2):
    r, c = lax.axis_index("row"), lax.axis_index("col")
    rows = codes_ref.shape[0]
    width = h_in.shape[3]
    pairs = CHUNK_TILES * HALF
    h_high, h_low = (high0, high1), (low0, low1)
    cols = [lax.rem(c + d, n_col) for d in range(n_col)]
    lines = [lax.rem(r + d, n_row) for d in range(n_row)]
    cube = Cube(n_col, lambda k, at: errors.at[k, rows_of(at, rows)], None, (hop_send, hop_recv, pair_send, pair_recv))

    def fetch(k, slot):
        def one(n, carry):
            for parity in range(2):
                pltpu.make_async_copy(
                    hessian_ref.at[rows_of(k, pairs), parity, n, 0],
                    h_in.at[slot, parity, :, rows_of(n, LANES)],
                    in_sem.at[slot],
                ).start()
            return carry

        lax.fori_loop(0, width // LANES, one, 0)

    def fetched(slot):
        pltpu.make_async_copy(h_in.at[slot], h_in.at[slot], in_sem.at[slot]).wait()

    def out_copies(k, slot):
        return [
            pltpu.make_async_copy(h_high[slot], high_out.at[k], out_sem.at[slot, 0]),
            pltpu.make_async_copy(h_low[slot], low_out.at[k], out_sem.at[slot, 1]),
        ]

    def convert(slot, columns):
        for parity in range(2):
            high, low = halves(h_in[slot, parity, :, columns])
            h_high[slot][parity * pairs : (parity + 1) * pairs, columns] = high
            h_low[slot][parity * pairs : (parity + 1) * pairs, columns] = low

    fetch(0, 0)
    if chunks > 1:
        fetch(1, 1)
    part_ref[...] = jnp.zeros_like(part_ref)
    maps_out[r, c] = padded_ref[...]
    greet([(r, cols[d]) for d in range(1, n_col)] + [(lines[d], c) for d in range(1, n_row)])

    span = max(run // 2, LANES)

    def piece(at):
        return codes_ref.at[:, rows_of(at * (run // 2) // span, span)]

    def send(src, dst, sends, recvs, d, device):
        return pltpu.make_async_remote_copy(
            src_ref=src, dst_ref=dst, send_sem=sends.at[d], recv_sem=recvs.at[d], device_id=device, device_id_type=MESH
        )

    here = spread_out.at[r, rows_of(c, rows)]
    spreads = [send(piece(cols[d]), here, code_send, code_recv, d, (r, cols[d])) for d in range(1, n_col)]
    maps = [send(padded_ref, maps_out.at[r, c], map_send, map_recv, d, (r, cols[d])) for d in range(1, n_col)]
    map_lines = [send(maps_out.at[r], maps_out.at[r], map_send2, map_recv2, d, (lines[d], c)) for d in range(1, n_row)]
    keep = pltpu.make_async_copy(piece(c), here, own_sem)

    def along(at, way):
        return pltpu.make_async_remote_copy(
            src_ref=spread_out.at[at],
            dst_ref=spread_out.at[at],
            send_sem=line_send.at[way, at],
            recv_sem=line_recv.at[way, at],
            device_id=(r + 1 - 2 * way, c),
            device_id_type=MESH,
        )

    def lines_start():
        for copy in maps + spreads:
            copy.wait_recv()
        keep.wait()
        for copy in map_lines:
            copy.start()

        @pl.when(r + 1 < n_row)
        def _():
            along(r, 0).start()

        @pl.when(r > 0)
        def _():
            along(r, 1).start()

    def lines_pass(d):
        @pl.when(r >= d)
        def _():
            along(r - d, 0).wait_recv()

            @pl.when(r + 1 < n_row)
            def _():
                along(r - d, 0).start()

        @pl.when(r + d < n_row)
        def _():
            along(r + d, 1).wait_recv()

            @pl.when(r > 0)
            def _():
                along(r + d, 1).start()

    def lines_drain():
        for copy in map_lines:
            copy.wait_recv()
        for copy in maps + spreads + map_lines:
            copy.wait_send()
        for d in range(n_row):
            @pl.when((r >= d) & (r + 1 < n_row))
            def _():
                along(r - d, 0).wait_send()

            @pl.when((r + d < n_row) & (r > 0))
            def _():
                along(r + d, 1).wait_send()

    def own(k, phase):
        for t in range(CHUNK_TILES):
            for i in range(rows // TILE_ROWS):
                at = pl.ds(i * TILE_ROWS, TILE_ROWS)
                j = k * CHUNK_TILES + t
                codes = codes_ref[at, rows_of(j, HALF)]
                even, odd = lookup(books_ref[map_ref[i, j]], codes)
                left = weights_ref[at, rows_of(2 * j, LANES)].astype(jnp.float32)
                right = weights_ref[at, rows_of(2 * j + 1, LANES)].astype(jnp.float32)
                w_even, w_odd = split_pairs(left, right)
                place = pl.ds(pl.multiple_of(c * rows + i * TILE_ROWS, TILE_ROWS), TILE_ROWS)
                errors[k, place, t * HALF : (t + 1) * HALF] = even - w_even
                errors[k, place, pairs + t * HALF : pairs + (t + 1) * HALF] = odd - w_odd
        cube.pass_on(k, 0, phase)

    def begin(k, phase):
        own(k, phase)
        if isinstance(k, int) and k == 0:
            for copy in spreads + maps + [keep]:
                copy.start()

    nt = min(width, 2048)

    def multiply(slot, columns):
        part_ref[:, columns] += three_products(e_high[...], e_low[...], h_high[slot][:, columns], h_low[slot][:, columns])

    def product(k, slot):
        step = 64

        @pl.when((k >= 0) & (k < chunks))
        def _():
            cube.pair_arrivals(k)

            def convert_error(n, carry):
                place = rows_of(n, step)
                e_high[place, :], e_low[place, :] = halves(errors[k, place, :])
                return carry

            lax.fori_loop(0, errors.shape[1] // step, convert_error, 0)

        @pl.when((k >= 0) & (k + 1 < chunks))
        def _():
            fetched(1 - slot)

            @pl.when(k >= 1)
            def _():
                for copy in out_copies(k - 1, 1 - slot):
                    copy.wait()

            def both(n, carry):
                columns = rows_of(n, nt)
                multiply(slot, columns)
                convert(1 - slot, columns)
                return carry

            lax.fori_loop(0, width // nt, both, 0)
            for copy in out_copies(k + 1, 1 - slot):
                copy.start()

            @pl.when(k + 3 < chunks)
            def _():
                fetch(k + 3, 1 - slot)

        @pl.when(k + 1 == chunks)
        def _():
            def alone(n, carry):
                multiply(slot, rows_of(n, nt))
                return carry

            lax.fori_loop(0, width // nt, alone, 0)

        @pl.when(k == -1)
        def _():
            lines_start()

        for d in range(1, n_row):
            @pl.when(k == (chunks - 1 if d + 1 == n_row else min(2 * d, chunks - 1)))
            def _():
                lines_pass(d)

    def convert_first(n, carry):
        convert(0, rows_of(n, nt))
        return carry

    def prepare():
        fetched(0)
        lax.fori_loop(0, width // nt, convert_first, 0)
        for copy in out_copies(0, 0):
            copy.start()
        if chunks > 2:
            fetch(2, 0)

    cube.turns(chunks, 0, 2, begin, product, prepare)
    for k in range(max(0, chunks - 2), chunks):
        for copy in out_copies(k, k % 2):
            copy.wait()
    lines_drain()
    cube.drain(chunks)


def first_product(n_row, n_col, tile_map, padded, codes, weights, books, hessian):
    rows, length = weights.shape
    count = hessian.shape[0]
    run = hessian.shape[2] * hessian.shape[3]
    width = hessian.shape[1] * run
    size = CHUNK_TILES * TILE_COLS
    chunks = count // size
    total_rows = rows * n_col
    chips = n_col // 2
    dma = pltpu.SemaphoreType.DMA
    whole = jax.ShapeDtypeStruct((chunks, size, width), jnp.bfloat16)
    block = pltpu.VMEM((size, width), jnp.bfloat16)
    return pl.pallas_call(
        functools.partial(first_kernel, n_row, n_col, chunks, run),
        in_specs=[SMEM, VMEM, VMEM, VMEM, VMEM, ANY],
        out_specs=[VMEM, ANY, ANY, ANY, VMEM],
        out_shape=[
            jax.ShapeDtypeStruct((total_rows, width), jnp.float32),
            whole,
            whole,
            jax.ShapeDtypeStruct((n_row, total_rows, max(run // 2, LANES)), jnp.int32),
            jax.ShapeDtypeStruct((n_row, n_col) + padded.shape, jnp.int32),
        ],
        scratch_shapes=[
            pltpu.VMEM((chunks, total_rows, size), jnp.float32),
            pltpu.VMEM((total_rows, size), jnp.bfloat16),
            pltpu.VMEM((total_rows, size), jnp.bfloat16),
            pltpu.VMEM((2, 2, size // 2, width), jnp.float32),
            block,
            block,
            block,
            block,
            dma((chunks, chips)),
            dma((chunks, chips)),
            dma((chunks, chips)),
            dma((chunks, chips)),
            dma((2,)),
            dma((2, 2)),
            dma((n_col,)),
            dma((n_col,)),
            dma,
            dma((2, n_row)),
            dma((2, n_row)),
            dma((n_col,)),
            dma((n_col,)),
            dma((n_row,)),
            dma((n_row,)),
        ],
        compiler_params=pltpu.CompilerParams(collective_id=1, has_side_effects=True, vmem_limit_bytes=VMEM_BYTES),
        cost_estimate=pl.CostEstimate(flops=6 * total_rows * width * count, bytes_accessed=8 * count * width, transcendentals=0),
        name="first_product",
    )(tile_map, padded, codes, weights, books.reshape(-1, 4, LANES), hessian.reshape(count // 2, 2, width // LANES, 1, LANES))


def next_kernel(n_col, chunks, down, map_ref, codes_ref, delta_ref, high_ref, low_ref, part_ref, codes_all, high0, high1, low0, low1, d_high0, d_high1, d_low0, d_low1, hop_send, hop_recv, pair_send, pair_recv, in_sem):
    r, c = lax.axis_index("row"), lax.axis_index("col")
    rows = codes_ref.shape[0]
    total_rows, width = part_ref.shape
    pairs = CHUNK_TILES * HALF
    h_high, h_low = (high0, high1), (low0, low1)
    d_high, d_low = (d_high0, d_high1), (d_low0, d_low1)
    cube = Cube(
        n_col,
        lambda k, at: codes_all.at[k, rows_of(at, rows)],
        lambda k: codes_ref.at[:, rows_of(k, pairs)],
        (hop_send, hop_recv, pair_send, pair_recv),
    )

    def fetch(k, slot):
        return [
            pltpu.make_async_copy(high_ref.at[k], h_high[slot], in_sem.at[slot, 0]),
            pltpu.make_async_copy(low_ref.at[k], h_low[slot], in_sem.at[slot, 1]),
        ]

    for k in range(min(2, chunks)):
        for copy in fetch(k, k):
            copy.start()
    part_ref[...] = jnp.zeros_like(part_ref)
    greet(
        [(r, flip(cube.chip, 1 << d) * 2 + cube.core) for d in range(cube.dims)] + [(r, cube.chip * 2 + 1 - cube.core)]
    )

    def own(k, phase):
        cube.pass_on(k, 0, phase)
        codes_all[k, rows_of(c, rows), :] = codes_ref[:, rows_of(k, pairs)]

    nt = min(width, 2048)
    tiles = total_rows // TILE_ROWS
    share = tiles // (width // nt)

    def look(k, slot, n):
        for q in range(share):
            i = n * share + q
            at = rows_of(i, TILE_ROWS)
            for t in range(CHUNK_TILES):
                codes = codes_all[k, at, t * HALF : (t + 1) * HALF]
                book = map_ref[r, i // down, lax.rem(i, down), k * CHUNK_TILES + t]
                for part, value in enumerate(lookup(delta_ref[book], codes)):
                    high, low = halves(value)
                    left = part * pairs + t * HALF
                    d_high[slot][at, left : left + HALF] = high
                    d_low[slot][at, left : left + HALF] = low

    def multiply(slot, n):
        columns = rows_of(n, nt)
        part_ref[:, columns] += three_products(
            d_high[slot][...], d_low[slot][...], h_high[slot][:, columns], h_low[slot][:, columns]
        )

    def loop(body):
        def one(n, carry):
            body(n)
            return carry

        lax.fori_loop(0, width // nt, one, 0)

    def work(k, slot):
        @pl.when((k >= 0) & (k < chunks))
        def _():
            cube.pair_arrivals(k)

        @pl.when((k >= 1) & (k <= chunks))
        def _():
            for copy in fetch(k - 1, 1 - slot):
                copy.wait()

        @pl.when(k == 0)
        def _():
            loop(lambda n: look(k, slot, n))

        @pl.when((k >= 1) & (k < chunks))
        def _():
            def body(n):
                multiply(1 - slot, n)
                look(k, slot, n)

            loop(body)

        @pl.when(k == chunks)
        def _():
            loop(lambda n: multiply(1 - slot, n))

        @pl.when((k >= 1) & (k + 1 < chunks))
        def _():
            for copy in fetch(k + 1, 1 - slot):
                copy.start()

    cube.turns(chunks, 1, 2, own, work)
    cube.drain(chunks)


def next_product(n_col, down, maps, codes, delta, high, low):
    chunks, size, width = high.shape
    rows = codes.shape[0]
    m = rows * n_col
    chips = n_col // 2
    dma = pltpu.SemaphoreType.DMA
    block = pltpu.VMEM((size, width), jnp.bfloat16)
    factor = pltpu.VMEM((m, size), jnp.bfloat16)
    return pl.pallas_call(
        functools.partial(next_kernel, n_col, chunks, down),
        in_specs=[SMEM, VMEM, VMEM, ANY, ANY],
        out_specs=VMEM,
        out_shape=jax.ShapeDtypeStruct((m, width), jnp.float32),
        scratch_shapes=[pltpu.VMEM((chunks, m, size // 2), jnp.int32)]
        + [block] * 4
        + [factor] * 4
        + [dma((chunks, chips))] * 4
        + [dma((2, 2))],
        compiler_params=pltpu.CompilerParams(collective_id=3, has_side_effects=True, vmem_limit_bytes=VMEM_BYTES),
        cost_estimate=pl.CostEstimate(flops=6 * m * width * size * chunks, bytes_accessed=4 * size * chunks * width, transcendentals=0),
        name="next_product",
    )(maps, codes, delta.reshape(-1, 4, LANES), high, low)


def spread_tile(codes, values):
    upper = codes // LOW
    lower = (codes & (LOW - 1)).astype(jnp.float32).astype(jnp.bfloat16)
    eight = lax.broadcasted_iota(jnp.int32, (8, LANES), 0)
    entry = lax.broadcasted_iota(jnp.int32, (LOW, LANES), 0).astype(jnp.float32).astype(jnp.bfloat16)
    one, zero = jnp.bfloat16(1), jnp.bfloat16(0)
    parts, hots = [], []
    for n in range(TILE_ROWS):
        fits = eight == upper[n : n + 1, :]
        part = jnp.concatenate([jnp.where(fits, x[n : n + 1, :], 0.0) for x in values], axis=0)
        parts.append(part.astype(jnp.bfloat16))
        hots.append(jnp.where(entry == lower[n : n + 1, :], one, zero))
    return lax.dot_general(
        jnp.concatenate(parts, axis=1), jnp.concatenate(hots, axis=1), NT, preferred_element_type=jnp.float32
    )


def scatter_kernel(run, gap, sizes, place_ref, map_ref, codes_ref, grad_ref, books_ref, sums_ref, planes_ref, order_ref):
    g = pl.program_id(0)
    groups, rows_here, span = codes_ref.shape
    down, across = rows_here // TILE_ROWS, groups * span // HALF
    map_down, map_across = sizes
    top = g * down
    begin = place_ref[0]
    halves_apart = run % TILE_COLS != 0
    row = lax.broadcasted_iota(jnp.int32, (8, LOW), 0)

    @pl.when(g == 0)
    def _():
        sums_ref[...] = jnp.zeros_like(sums_ref)
        source = lax.broadcasted_iota(jnp.int32, order_ref.shape, 0)
        target = lax.broadcasted_iota(jnp.int32, order_ref.shape, 1)
        wanted = jnp.where(target < HALF, 2 * target, 2 * (target - HALF) + 1)
        order_ref[...] = jnp.where(source == wanted, 1.0, 0.0).astype(jnp.bfloat16)

    def part(j, carry):
        columns = rows_of(j, TILE_COLS)
        both = jnp.concatenate(halves(grad_ref[:, columns]), axis=0)
        planes_ref[:, columns] = jnp.dot(both, order_ref[...], preferred_element_type=jnp.float32)
        return carry

    lax.fori_loop(0, across, part, 0)

    def book(i, column):
        line = top + i
        tile = ((column // run) * gap + begin + column % run) // TILE_COLS
        return map_ref[tile // map_across, line // map_down, line % map_down, tile % map_across]

    def add(index, sums):
        even, odd = sums[0:8] + sums[8:16], sums[16:24] + sums[24:32]
        first = jnp.where(row < 4, even, jnp.concatenate([odd[4:8], odd[0:4]], axis=0))
        second = jnp.where(row < 4, jnp.concatenate([even[4:8], even[0:4]], axis=0), odd)
        sums_ref[rows_of(index, BOOK_LINES), 0:LOW] += jnp.concatenate([first, second], axis=0)

    def tile(t, carry):
        i, j = t // across, t % across
        rows = rows_of(i, TILE_ROWS)
        codes = codes_ref[j // (span // HALF), rows, rows_of(j % (span // HALF), HALF)]
        low_rows = pl.ds(pl.multiple_of(rows_here + i * TILE_ROWS, TILE_ROWS), TILE_ROWS)
        values = [planes_ref[at, rows_of(2 * j + odd, HALF)] for odd in range(2) for at in (rows, low_rows)]
        if halves_apart:
            left = lax.broadcasted_iota(jnp.int32, codes.shape, 1) < HALF // 2
            add(book(i, j * TILE_COLS), spread_tile(codes, [jnp.where(left, x, 0.0) for x in values]))
            add(book(i, j * TILE_COLS + LANES), spread_tile(codes, [jnp.where(left, 0.0, x) for x in values]))
        else:
            add(book(i, j * TILE_COLS), spread_tile(codes, values))
        return carry

    lax.fori_loop(0, down * across, tile, 0, unroll=1 if halves_apart else 8)

    @pl.when(g == pl.num_programs(0) - 1)
    def _():
        groups = LANES // LOW
        size = 64

        def squeeze(n, carry):
            at = pl.multiple_of(n * size * groups, size * groups)
            total = sums_ref[pl.ds(at, size, stride=groups), :]
            for b in range(1, groups):
                total = total + pltpu.roll(sums_ref[pl.ds(at + b, size, stride=groups), :], b * LOW, 1)
            books_ref[rows_of(n, size), :] = total
            return carry

        lax.fori_loop(0, books_ref.shape[0] // size, squeeze, 0)


def scatter(run, gap, sizes, begin, maps, codes, grad, shape):
    m, n = grad.shape
    block = min(m, 128)
    return pl.pallas_call(
        functools.partial(scatter_kernel, run, gap, sizes),
        grid=(m // block,),
        in_specs=[
            SMEM,
            SMEM,
            pl.BlockSpec((codes.shape[0], block, codes.shape[2]), lambda i: (0, i, 0)),
            pl.BlockSpec((block, n), lambda i: (i, 0)),
        ],
        out_specs=pl.BlockSpec(shape, lambda i: (0, 0)),
        out_shape=jax.ShapeDtypeStruct(shape, jnp.float32),
        scratch_shapes=[
            pltpu.VMEM((shape[0] // 4 * BOOK_LINES, LANES), jnp.float32),
            pltpu.VMEM((2 * block, n), jnp.float32),
            pltpu.VMEM((TILE_COLS, TILE_COLS), jnp.bfloat16),
        ],
        compiler_params=pltpu.CompilerParams(vmem_limit_bytes=VMEM_BYTES),
        cost_estimate=pl.CostEstimate(flops=64 * 32 * m * n, bytes_accessed=6 * m * n, transcendentals=0),
        name="scatter",
    )(begin, maps, codes, grad)


def update_kernel(n_row, n_col, parts, grad_ref, out_ref, pair_in, pair_sum, chip_in, chip_sum, row_in, *sems):
    r, c = lax.axis_index("row"), lax.axis_index("col")
    chip, core = c // 2, lax.rem(c, 2)
    chips = n_col // 2
    length = grad_ref.shape[0] // parts
    half = length // 2
    wide = half // chips
    thin = wide // n_row
    pair = (r, chip * 2 + 1 - core)
    others = [lax.rem(chip + d, chips) for d in range(chips)]
    lines = [lax.rem(r + d, n_row) for d in range(n_row)]
    greet(
        [pair]
        + [(r, others[d] * 2 + core) for d in range(1, chips)]
        + [(lines[d], c) for d in range(1, n_row)]
    )
    started = []

    def send(src, dst, stage, q, d, device):
        copy = pltpu.make_async_remote_copy(
            src_ref=src,
            dst_ref=dst,
            send_sem=sems[2 * stage].at[q, d],
            recv_sem=sems[2 * stage + 1].at[q, d],
            device_id=device,
            device_id_type=MESH,
        )
        copy.start()
        started.append(copy)
        return copy

    def part(q, index, size):
        return pl.ds(pl.multiple_of(q * length + index * size, size), size)

    def received(copies):
        for copy in copies:
            copy.wait_recv()

    def swap(q, before):
        return [send(grad_ref.at[part(q, 1 - core, half)], pair_in.at[q], 0, q, 0, pair)]

    def over_chips(q, before):
        received(before)
        pair_sum[q] = grad_ref[part(q, core, half), :] + pair_in[q]
        return [
            send(pair_sum.at[q, rows_of(others[d], wide)], chip_in.at[q, d], 1, q, d, (r, others[d] * 2 + core))
            for d in range(1, chips)
        ]

    def over_rows(q, before):
        received(before)
        total = pair_sum[q, rows_of(chip, wide), :]
        for d in range(1, chips):
            total = total + chip_in[q, d]
        chip_sum[q] = total
        return [
            send(chip_sum.at[q, rows_of(lines[d], thin)], row_in.at[q, d], 2, q, d, (lines[d], c))
            for d in range(1, n_row)
        ]

    def change(q, before):
        received(before)
        total = chip_sum[q, rows_of(r, thin), :]
        for d in range(1, n_row):
            total = total + row_in[q, d]
        mine = part(q, (core * chips + chip) * n_row + r, thin)
        out_ref[mine, :] = -learn_rate * (2.0 * total)
        return [send(out_ref.at[mine], out_ref.at[mine], 3, q, d, (lines[d], c)) for d in range(1, n_row)]

    def to_chips(q, before):
        received(before)
        piece = part(q, core * chips + chip, wide)
        return [
            send(out_ref.at[piece], out_ref.at[piece], 4, q, d, (r, others[d] * 2 + core)) for d in range(1, chips)
        ]

    def to_pair(q, before):
        received(before)
        piece = part(q, core, half)
        return [send(out_ref.at[piece], out_ref.at[piece], 5, q, 0, pair)]

    before = [[] for _ in range(parts)]
    for stage in (swap, over_chips, over_rows, change, to_chips, to_pair):
        for q in range(parts):
            before[q] = stage(q, before[q])
    for copies in before:
        received(copies)
    for copy in started:
        copy.wait_send()


def update(n_row, n_col, grad):
    chips = n_col // 2
    parts = 4 if grad.shape[0] % (4 * 2 * chips * n_row * 8) == 0 else 2
    half = grad.shape[0] // parts // 2
    wide = half // chips
    thin = wide // n_row
    dma = pltpu.SemaphoreType.DMA
    sizes = [1, chips, n_row, n_row, chips, 1]
    return pl.pallas_call(
        functools.partial(update_kernel, n_row, n_col, parts),
        in_specs=[VMEM],
        out_specs=VMEM,
        out_shape=jax.ShapeDtypeStruct(grad.shape, jnp.float32),
        scratch_shapes=[
            pltpu.VMEM((parts, half, LANES), jnp.float32),
            pltpu.VMEM((parts, half, LANES), jnp.float32),
            pltpu.VMEM((parts, chips, wide, LANES), jnp.float32),
            pltpu.VMEM((parts, wide, LANES), jnp.float32),
            pltpu.VMEM((parts, n_row, thin, LANES), jnp.float32),
        ]
        + [dma((parts, size)) for size in sizes for _ in range(2)],
        compiler_params=pltpu.CompilerParams(collective_id=0, has_side_effects=True),
        name="update",
    )(grad)


def per_device(n_row, n_col, hessian, weights, codes, tile_map, codebooks):
    count, parts, entries = codebooks.shape
    books = codebooks.reshape(count, parts, entries // LANES, LANES).transpose(0, 2, 1, 3).reshape(-1, LANES)
    run = hessian.shape[2] * hessian.shape[3]
    c = lax.axis_index("col")
    begin = jnp.full((1,), c * run, jnp.int32)
    down, across = tile_map.shape
    padded = jnp.pad(tile_map, ((0, -down % 8), (0, -across % LANES)))

    grad, high, low, spread, maps = first_product(n_row, n_col, tile_map, padded, codes, weights, books, hessian)
    if run // 2 < spread.shape[2]:
        groups, m, span = spread.shape
        spread = lax.dynamic_slice(spread, (0, 0, lax.rem(c * (run // 2), span)), (groups, m, run // 2))
        spread = spread.transpose(1, 0, 2).reshape(1, m, groups * (run // 2))
    split = functools.partial(scatter, run, n_col * run, (down, across), begin, maps, spread)
    delta = update(n_row, n_col, split(grad, books.shape))
    grad = next_product(n_col, down, maps, codes, delta, high, low)
    books = books + (2.0 * delta + update(n_row, n_col, split(grad, books.shape)))
    return books.reshape(count, entries // LANES, parts, LANES).transpose(0, 2, 1, 3).reshape(codebooks.shape)


def solution(mesh):
    placed = (P("row", None, "col", None), P("col", "row"), P("col", "row"), P("col", "row"), P())
    body = functools.partial(per_device, mesh.shape["row"], mesh.shape["col"])
    return jax.shard_map(body, mesh=mesh, in_specs=placed, out_specs=P(), check_vma=False)
```
